32 devices in a mesh: groups: 2 (over y), frames: 16 (over z, x, core).
Axes of the slice: x: 2, y: 2, z: 4, core: 2. Of those that a mesh axis runs over, the one named last changes fastest.
Arguments:
- video_frames: bfloat16 [64, 1024, 1024], P(('groups', 'frames')), parts along dimension 0, may hold values from -6 to 6
- segments: int32 [64], P('groups'), parts along dimension 0, may hold values from 0 to 3, never falling along the last dimension, each value on 1 to 29 neighbouring positions
- ref_pick: int32 [8], P('groups'), parts along dimension 0, may hold values from 0 to 4095
- band_taps: bfloat16 [32], replicated, may hold values from -2 to 2
Outputs:
- motion: float32 [64, 256, 256], P(('groups', 'frames')), parts along dimension 0
The draws below stay inside these ranges and needn't reach their ends.
There are 2 independent parts, one for each index of `groups`. The reference program is written for one: setup_inputs(seed, part) draws one part's arguments, and reference() takes and returns one part's arrays. A program takes and returns all parts, laid end to end along the dimension named above; an argument that names none is the same for every part. Nothing has to cross between parts.
Inputs may be any that keep to these rules, and one draw needn't show every extreme that they name: Segment numbers never fall along the frames; each of the 4 segments holds 1 to 29 frames and one holds exactly 29.
All inputs are finite; a program needn't handle non-finite values.
Results may differ from the reference program's by a relative error of at most 0.012.
Values may be sent and summed in bfloat16 or wider, within the bound.
A program may use at most 128 MiB of HBM per device.

```python
import math
import jax
import jax.numpy as jnp
import numpy as np
from jax import lax

IMG = 1024
ORIENT = 4
TAPS = 32
NSEG = 4
QUART = 256
FRAMES = 32
SEG_MOST = 29


def plant(values, key, least, high):
    longest = values.shape.index(max(values.shape))
    spots = []
    for shift in (0, 1):
        where = [jax.random.randint(jax.random.fold_in(key, axis), (), 0, length) for axis, length in enumerate(values.shape)]
        where[longest] = (where[longest] + shift) % values.shape[longest]
        spots.append(tuple(where))
    return values.at[spots[0]].set(least).at[spots[1]].set(high)


def block_scale(stream_key, dims, shards, low, high):
    def one(dim, parts):
        draws = jax.random.uniform(jax.random.fold_in(jax.random.fold_in(stream_key, 6), dim), (parts,), jnp.float32, low / len(shards), high / len(shards))
        return jnp.repeat(jnp.exp(draws), dims[dim] // parts).reshape((-1,) + (1,) * (len(dims) - dim - 1))

    factor_of = one(*shards[0])
    for cut in shards[1:]:
        factor_of = factor_of * one(*cut)
    return factor_of


def length_profile(number_of, total, limit, lean):
    portions = [(1 << 20) // math.isqrt(rank ** lean) + 1 for rank in range(2, number_of + 1)]
    rest, holding = total - limit - (number_of - 1), [1] * (number_of - 1)
    while rest > 0:
        free = [i for i in range(number_of - 1) if holding[i] < limit]
        mass, remaining = sum([portions[i] for i in free]), rest
        for i in free:
            more = min(limit - holding[i], max(1, remaining * portions[i] // mass), rest)
            holding[i] = holding[i] + more
            rest = rest - more
    return np.array([limit] + holding)


def ragged(rng, amount, total, reach, slope):
    if amount == 2:
        one = jax.random.randint(rng, (), max(1, total - reach), min(reach, total - 1) + 1)
        return jnp.stack([one, total - one])
    tallies = jnp.asarray(length_profile(amount, total, reach, slope), jnp.int32)
    couples = (amount - 1) // 2
    source_of, receiver = tallies[1:1 + 2 * couples:2], tallies[2:2 + 2 * couples:2]
    slack = jnp.minimum(source_of - 1, reach - receiver)
    moved = jax.random.randint(jax.random.fold_in(rng, 1), (couples,), 0, 1 << 20) % (slack + 1)
    tallies = tallies.at[1:1 + 2 * couples:2].set(source_of - moved).at[2:2 + 2 * couples:2].set(receiver + moved)
    return tallies[jax.random.permutation(jax.random.fold_in(rng, 2), amount)]


def scatter_about(stream_key, extent, width, bound, cuts=(), held_as=jnp.bfloat16):
    result = width * jax.random.normal(stream_key, extent, jnp.float32)
    if cuts:
        result = result * block_scale(stream_key, extent, cuts, -0.22, 0.18)
    return jnp.clip(result, -bound, bound).astype(held_as)


def setup_inputs(seed: int = 0, part: int = 0) -> dict:
    seeds = jax.random.split(jax.random.key(seed), 5)
    part_keys = jax.random.split(jax.random.fold_in(seeds[4], part), 5)
    return {
        "video_frames": scatter_about(part_keys[0], (FRAMES, IMG, IMG), 1.0, 6.0, ((0, 16),)),
        "segments": jnp.searchsorted(jnp.cumsum(ragged(part_keys[1], NSEG, FRAMES, SEG_MOST, 1)), jnp.arange(FRAMES), side="right").astype(jnp.int32),
        "ref_pick": plant(jax.random.randint(part_keys[2], (NSEG,), 0, 4096), jax.random.fold_in(part_keys[2], 1), 0, 4095).astype(jnp.int32),
        "band_taps": scatter_about(seeds[3], (TAPS,), 0.35, 2.0),
    }


blur_sigma = 2.0
gabor_sigma = 2.0
wave_number = math.pi / 2.0
gabor_gain = 2.0

def make_down(full_size, quarter):
    position = jnp.arange(quarter, dtype=jnp.float32)[:, None]
    columns = jnp.arange(full_size, dtype=jnp.float32)[None, :]
    offset_grid = columns - 4.0 * position - 1.5
    weight = jnp.exp(-offset_grid * offset_grid / (2.0 * blur_sigma * blur_sigma))
    return (weight / lax.optimization_barrier(jnp.sum(weight, axis=1, keepdims=True))).astype(jnp.bfloat16)

def gabor_tables(quarter, orient):
    position = jnp.arange(quarter, dtype=jnp.float32)
    offset_grid = position[None, :] - position[:, None]
    envelope = gabor_gain * jnp.exp(-offset_grid * offset_grid / (2.0 * gabor_sigma * gabor_sigma))
    angles = jnp.arange(orient, dtype=jnp.float32) * (math.pi / orient)
    wave_x = wave_number * jnp.cos(angles)
    wave_y = wave_number * jnp.sin(angles)
    phase_y = wave_y[:, None, None] * offset_grid[None]
    left_table = jnp.stack([envelope * jnp.cos(phase_y), envelope * jnp.sin(phase_y)], axis=2)
    left_table = left_table.reshape(orient * quarter * 2, quarter).astype(jnp.bfloat16)
    phase_x = wave_x[:, None, None] * (-offset_grid)[None]
    real_part = envelope * jnp.cos(phase_x)
    imag_part = envelope * jnp.sin(phase_x)
    upper_half = jnp.concatenate([real_part, imag_part], axis=2)
    lower_half = jnp.concatenate([-imag_part, real_part], axis=2)
    right_table = jnp.concatenate([upper_half, lower_half], axis=1).astype(jnp.bfloat16)
    return (left_table, right_table)

def frame_coeff(single, down_matrix, left_table, right_table):
    half_done = jnp.dot(single, down_matrix.T, preferred_element_type=jnp.float32).astype(jnp.bfloat16)
    reduced = jnp.dot(down_matrix, half_done, preferred_element_type=jnp.float32).astype(jnp.bfloat16)
    stacked = jnp.dot(left_table, reduced, preferred_element_type=jnp.float32).astype(jnp.bfloat16)
    quarter = reduced.shape[0]
    orient = right_table.shape[0]
    stacked = stacked.reshape(orient, quarter, 2 * quarter)
    return jnp.einsum('oya,oab->oyb', stacked.astype(jnp.float32), right_table.astype(jnp.float32)).astype(jnp.bfloat16)

def phase_terms(coeffs, per_frame):
    quarter = coeffs.shape[-1] // 2
    coeff_real = coeffs[..., :quarter].astype(jnp.float32)
    coeff_imag = coeffs[..., quarter:].astype(jnp.float32)
    ref_real = per_frame[..., :quarter].astype(jnp.float32)
    ref_imag = per_frame[..., quarter:].astype(jnp.float32)
    prod_real = coeff_real * ref_real + coeff_imag * ref_imag
    prod_imag = coeff_imag * ref_real - coeff_real * ref_imag
    phase_signal = (prod_imag / jnp.sqrt(prod_real * prod_real + prod_imag * prod_imag + 1.0)).astype(jnp.bfloat16)
    amplitude = coeff_real * coeff_real + coeff_imag * coeff_imag
    return (phase_signal, amplitude)

def taps_matrix(band_taps, frame_count):
    frame_index = jnp.arange(frame_count, dtype=jnp.int32)
    lag_grid = frame_index[:, None] - frame_index[None, :]
    one_hot = (lag_grid[:, :, None] == jnp.arange(band_taps.shape[0], dtype=jnp.int32)[None, None, :]).astype(jnp.float32)
    return jnp.einsum('tsk,k->ts', one_hot, band_taps.astype(jnp.float32)).astype(jnp.bfloat16)

def segment_refs(segments, ref_pick, segment_count):
    numbers = jnp.arange(segment_count, dtype=jnp.int32)
    starts = lax.optimization_barrier(jnp.sum((segments[None, :] < numbers[:, None]).astype(jnp.int32), axis=1))
    counts = lax.optimization_barrier(jnp.sum((segments[None, :] == numbers[:, None]).astype(jnp.int32), axis=1))
    return (starts + ref_pick % counts).astype(jnp.int32)

def reference(video_frames, segments, ref_pick, band_taps):
    down_matrix = make_down(IMG, QUART)
    left_table, right_table = gabor_tables(QUART, ORIENT)
    coeffs = lax.map(lambda single: frame_coeff(single, down_matrix, left_table, right_table), video_frames)
    ref_frames = segment_refs(segments, ref_pick, NSEG)
    ref_coeffs = coeffs[ref_frames]
    per_frame = ref_coeffs[segments]
    phase_signal, amplitude = phase_terms(coeffs, per_frame)
    matrix = taps_matrix(band_taps, FRAMES)
    filtered = jnp.dot(matrix, phase_signal.reshape(FRAMES, -1), preferred_element_type=jnp.float32)
    filtered = filtered.astype(jnp.bfloat16).reshape(phase_signal.shape).astype(jnp.float32)
    return lax.optimization_barrier(jnp.sum(amplitude * filtered, axis=1)) / (lax.optimization_barrier(jnp.sum(amplitude, axis=1)) + 1.0)
```

```python
import math

import jax
import numpy as np
import jax.numpy as jnp
from jax import lax
from jax.experimental import pallas as pl
from jax.experimental.pallas import tpu as pltpu
from jax.sharding import PartitionSpec as P

IMG = 1024
ORIENT = 4
NSEG = 4
QUART = 256


blur_sigma = 2.0
gabor_sigma = 2.0
wave_number = math.pi / 2.0
gabor_gain = 2.0


def spread(x, axis, root):
    mine = lax.axis_index(axis) == root
    return lax.psum(jnp.where(mine, x, jnp.zeros_like(x)), axis)


def make_down(full_size, quarter):
    position = jnp.arange(quarter, dtype=jnp.float32)[:, None]
    columns = jnp.arange(full_size, dtype=jnp.float32)[None, :]
    offset_grid = columns - 4.0 * position - 1.5
    weight = jnp.exp(-offset_grid * offset_grid / (2.0 * blur_sigma * blur_sigma))
    return (weight / jnp.sum(weight, axis=1, keepdims=True)).astype(jnp.bfloat16)


def gabor_tables(quarter, orient):
    position = jnp.arange(quarter, dtype=jnp.float32)
    offset_grid = position[None, :] - position[:, None]
    envelope = gabor_gain * jnp.exp(-offset_grid * offset_grid / (2.0 * gabor_sigma * gabor_sigma))
    angles = jnp.arange(orient, dtype=jnp.float32) * (math.pi / orient)
    wave_x = wave_number * jnp.cos(angles)
    wave_y = wave_number * jnp.sin(angles)
    phase_y = wave_y[:, None, None] * offset_grid[None]
    left_table = jnp.stack([envelope * jnp.cos(phase_y), envelope * jnp.sin(phase_y)], axis=2)
    left_table = left_table.reshape(orient * quarter * 2, quarter).astype(jnp.bfloat16)
    phase_x = wave_x[:, None, None] * (-offset_grid)[None]
    real_part = envelope * jnp.cos(phase_x)
    imag_part = envelope * jnp.sin(phase_x)
    upper_half = jnp.concatenate([real_part, imag_part], axis=2)
    lower_half = jnp.concatenate([-imag_part, real_part], axis=2)
    right_table = jnp.concatenate([upper_half, lower_half], axis=1).astype(jnp.bfloat16)
    return (left_table, right_table)


def phase_terms(coeffs, per_frame):
    quarter = coeffs.shape[-1] // 2
    coeff_real = coeffs[..., :quarter].astype(jnp.float32)
    coeff_imag = coeffs[..., quarter:].astype(jnp.float32)
    ref_real = per_frame[..., :quarter].astype(jnp.float32)
    ref_imag = per_frame[..., quarter:].astype(jnp.float32)
    prod_real = coeff_real * ref_real + coeff_imag * ref_imag
    prod_imag = coeff_imag * ref_real - coeff_real * ref_imag
    phase_signal = (
        prod_imag / jnp.sqrt(prod_real * prod_real + prod_imag * prod_imag + 1.0)
    ).astype(jnp.bfloat16)
    amplitude = coeff_real * coeff_real + coeff_imag * coeff_imag
    return (phase_signal, amplitude)


def taps_matrix(band_taps, frame_count):
    frame_index = jnp.arange(frame_count, dtype=jnp.int32)
    lag_grid = frame_index[:, None] - frame_index[None, :]
    one_hot = (
        lag_grid[:, :, None] == jnp.arange(band_taps.shape[0], dtype=jnp.int32)[None, None, :]
    ).astype(jnp.float32)
    return jnp.einsum("tsk,k->ts", one_hot, band_taps.astype(jnp.float32)).astype(jnp.bfloat16)


def segment_refs(segments, ref_pick, segment_count):
    numbers = jnp.arange(segment_count, dtype=jnp.int32)
    starts = jnp.sum((segments[None, :] < numbers[:, None]).astype(jnp.int32), axis=1)
    counts = jnp.sum((segments[None, :] == numbers[:, None]).astype(jnp.int32), axis=1)
    return starts + ref_pick % counts


def body(video_frames, segments, ref_pick, band_taps):
    frames_here = video_frames.shape[0]
    down_matrix = make_down(IMG, QUART)
    left_table, right_table = gabor_tables(QUART, ORIENT)

    def reduce_frames(pictures):
        half_done = jnp.einsum(
            "nia,qa->niq", pictures, down_matrix, preferred_element_type=jnp.float32
        ).astype(jnp.bfloat16)
        return jnp.einsum(
            "qi,nik->nqk", down_matrix, half_done, preferred_element_type=jnp.float32
        ).astype(jnp.bfloat16)

    def filter_frames(reduced):
        stacked = jnp.einsum(
            "ra,nak->nrk", left_table, reduced, preferred_element_type=jnp.float32
        ).astype(jnp.bfloat16)
        stacked = stacked.reshape(reduced.shape[0], ORIENT, QUART, 2 * QUART)
        return jnp.einsum(
            "noya,oab->noyb", stacked, right_table, preferred_element_type=jnp.float32
        ).astype(jnp.bfloat16)

    small_own = reduce_frames(video_frames)
    coeff_own = filter_frames(small_own)
    ref_frames = segment_refs(segments, ref_pick, NSEG)
    gathered = []
    for segment in range(NSEG):
        root_index = ref_frames[segment] // frames_here
        local_index = ref_frames[segment] % frames_here
        payload = lax.dynamic_index_in_dim(video_frames, local_index, 0, keepdims=False)
        gathered.append(spread(payload, "frames", root_index))
    ref_coeff = filter_frames(reduce_frames(jnp.stack(gathered)))
    first_frame = lax.axis_index("frames") * frames_here
    own_ids = lax.dynamic_slice_in_dim(segments, first_frame, frames_here)
    select = (own_ids[:, None] == jnp.arange(NSEG, dtype=jnp.int32)[None, :]).astype(jnp.bfloat16)
    per_frame = jnp.dot(select, ref_coeff.reshape(NSEG, -1), preferred_element_type=jnp.float32)
    per_frame = per_frame.astype(jnp.bfloat16).reshape(coeff_own.shape)
    phase_signal, amplitude = phase_terms(coeff_own, per_frame)
    phase_signal = phase_signal.reshape(frames_here, ORIENT, QUART * QUART)
    pixel_rows = lax.all_to_all(phase_signal, "frames", split_axis=2, concat_axis=0, tiled=True)
    matrix = taps_matrix(band_taps, pixel_rows.shape[0])
    filtered = jnp.einsum(
        "ts,sop->top", matrix, pixel_rows, preferred_element_type=jnp.float32
    ).astype(jnp.bfloat16)
    filtered = lax.all_to_all(filtered, "frames", split_axis=0, concat_axis=2, tiled=True)
    filtered = filtered.reshape(frames_here, ORIENT, QUART, QUART).astype(jnp.float32)
    return jnp.sum(amplitude * filtered, axis=1) / (jnp.sum(amplitude, axis=1) + 1.0)


PICK_LIMIT = 4096
REACH = 32


def down_table():
    position = np.arange(QUART, dtype=np.float32)[:, None]
    columns = np.arange(IMG, dtype=np.float32)[None, :]
    offset = columns - np.float32(4.0) * position - np.float32(1.5)
    weight = np.exp(-offset * offset / np.float32(2.0 * blur_sigma * blur_sigma))
    return (weight / np.sum(weight, axis=1, keepdims=True)).astype(jnp.bfloat16)


def waves():
    angles = np.arange(ORIENT, dtype=np.float32) * np.float32(math.pi / ORIENT)
    return np.float32(wave_number) * np.cos(angles), np.float32(wave_number) * np.sin(angles)


def gabor_envelope(offset):
    return np.float32(gabor_gain) * np.exp(-offset * offset / np.float32(2.0 * gabor_sigma * gabor_sigma))


def left_window(rows):
    offset = (
        np.arange(rows + 2 * REACH, dtype=np.float32)[None, :]
        - REACH
        - np.arange(rows, dtype=np.float32)[:, None]
    )
    envelope = gabor_envelope(offset)
    phase = waves()[1][:, None, None] * offset[None]
    table = np.stack([envelope * np.cos(phase), envelope * np.sin(phase)], axis=1)
    return table.reshape(ORIENT * 2 * rows, -1).astype(jnp.bfloat16)


def right_tables():
    position = np.arange(QUART, dtype=np.float32)
    offset = position[:, None] - position[None, :]
    envelope = gabor_envelope(offset)
    phase = waves()[0][:, None, None] * offset[None]
    real, imag = envelope * np.cos(phase), envelope * np.sin(phase)
    upper = np.concatenate([real, imag], axis=2)
    lower = np.concatenate([-imag, real], axis=2)
    return np.stack([upper, lower], axis=1).astype(jnp.bfloat16)


PLANE = 4
PAIR = 2
LAG = 3


def flip(number, bits):
    step = 1
    while step <= bits:
        if bits & step:
            number = number + step - 2 * step * ((number // step) % 2)
        step *= 2
    return number


def make_kernel(parts, here, rows):
    frames = parts * here
    planes = parts // PLANE
    window = rows + 2 * REACH
    pair_window = PAIR * rows + 2 * REACH
    total = frames * rows
    chunks = 2

    def kernel(
        segments, picks, taps, video_hbm, down_hbm, down_t_hbm, left, right_hbm, out_hbm,
        video, down, down_t, right, half, column, beside, twin, stacked, coeffs,
        phase, matrix, numer, denom, moved,
        load_sem, store_sem, send_z, recv_z, send_x, recv_x, send_c, recv_c, send_b, recv_b,
    ):
        me = lax.axis_index("frames")
        plane, spot = me // PLANE, me % PLANE
        across, sibling = flip(spot, PAIR), flip(spot, 1)
        side, core = spot // PAIR, spot % PAIR
        barrier = pltpu.get_barrier_semaphore()

        def peer(j):
            return lax.rem(me + j, parts)

        def piece(n, part):
            height = IMG // chunks
            where = pl.ds(part * height, height)
            return pltpu.make_async_copy(
                video_hbm.at[n, where], video.at[n, where], load_sem.at[3 + n * chunks + part]
            )

        load_down_t = pltpu.make_async_copy(down_t_hbm, down_t, load_sem.at[0])
        load_down = pltpu.make_async_copy(down_hbm, down, load_sem.at[1])
        load_right = pltpu.make_async_copy(right_hbm, right, load_sem.at[2])
        load_down_t.start()
        for n in range(here):
            for part in range(chunks):
                piece(n, part).start()
            if n == 0:
                load_down.start()
        load_right.start()

        below, above = plane > 0, plane < planes - 1

        def greet(where):
            pl.semaphore_signal(barrier, inc=1, device_id={"frames": where})

        greet(plane * PLANE + sibling)
        greet(plane * PLANE + across)

        @pl.when(below)
        def _():
            greet(me - PLANE)

        @pl.when(above)
        def _():
            greet(me + PLANE)

        blank = jnp.zeros((planes * here, REACH, QUART), jnp.bfloat16)
        column[:, :REACH, :] = blank
        column[:, REACH + QUART :, :] = blank

        block = PLANE * rows
        low, high = REACH, REACH + QUART

        def z_copy(up, f, n, q):
            first, last = (block * (q + 1), high) if up else (low, block * q + 2 * REACH)
            part = column.at[f * here + n, first:last, :]
            way = 0 if up else 1
            return pltpu.make_async_remote_copy(
                src_ref=part,
                dst_ref=part,
                send_sem=send_z.at[way, f, n],
                recv_sem=recv_z.at[way, f, n],
                device_id={"frames": me + (PLANE if up else -PLANE)},
            )

        def z_each(up, f, n, act, receive=False):
            for q in range(planes - 1) if up else range(1, planes):
                here_if = q if not receive else (q + 1 if up else q - 1)

                @pl.when(plane == here_if)
                def _():
                    act(z_copy(up, f, n, q))

        def x_copy(f, n):
            first = pl.multiple_of(plane * block + (1 - side) * PAIR * rows, rows)
            return pltpu.make_async_remote_copy(
                src_ref=column.at[f * here + n, pl.ds(first, pair_window), :],
                dst_ref=beside.at[f * here + n],
                send_sem=send_x.at[f, n],
                recv_sem=recv_x.at[f, n],
                device_id={"frames": plane * PLANE + across},
            )

        def core_copy(f, n):
            first = pl.multiple_of(plane * block + sibling * rows, rows)
            return pltpu.make_async_remote_copy(
                src_ref=column.at[f * here + n, pl.ds(first, window), :],
                dst_ref=twin.at[0, f * here + n],
                send_sem=send_c.at[0, f, n],
                recv_sem=recv_c.at[0, f, n],
                device_id={"frames": plane * PLANE + sibling},
            )

        def pass_copy(f, n):
            first = pl.multiple_of((1 - core) * rows, rows)
            return pltpu.make_async_remote_copy(
                src_ref=beside.at[f * here + n, pl.ds(first, window), :],
                dst_ref=twin.at[1, f * here + n],
                send_sem=send_c.at[1, f, n],
                recv_sem=recv_c.at[1, f, n],
                device_id={"frames": plane * PLANE + sibling},
            )

        def spread_sideways(f, n):
            x_copy(f, n).start()
            core_copy(f, n).start()

        load_down_t.wait()
        for n in range(here):
            for part in range(chunks):
                piece(n, part).wait()
                where = slice(part * (IMG // chunks), (part + 1) * (IMG // chunks))
                half[n, where] = jnp.dot(
                    video[n, where], down_t[...], preferred_element_type=jnp.float32
                ).astype(jnp.bfloat16)
            if n == 0:
                load_down.wait()
            column[plane * here + n, REACH : REACH + QUART, :] = jnp.dot(
                down[...], half[n], preferred_element_type=jnp.float32
            ).astype(jnp.bfloat16)
            if n == 0:
                pl.semaphore_wait(
                    barrier, 2 + jnp.where(below, 1, 0) + jnp.where(above, 1, 0)
                )
            z_each(True, plane, n, lambda copy: copy.start())
            z_each(False, plane, n, lambda copy: copy.start())
            spread_sideways(plane, n)

        lag = lax.broadcasted_iota(jnp.int32, (frames, frames), 0) - lax.broadcasted_iota(
            jnp.int32, (frames, frames), 1
        )
        toeplitz = jnp.zeros((frames, frames), jnp.float32)
        tap_row = taps[...].astype(jnp.float32)
        for k in range(min(taps.shape[1], frames)):
            toeplitz = jnp.where(lag == k, tap_row[:, k : k + 1], toeplitz)
        owner = lax.broadcasted_iota(jnp.int32, (total, frames), 0) // rows
        repeat = jnp.where(
            owner == lax.broadcasted_iota(jnp.int32, (total, frames), 1), 1.0, 0.0
        ).astype(jnp.bfloat16)
        tall = jnp.dot(
            repeat, toeplitz.astype(jnp.bfloat16), preferred_element_type=jnp.float32
        ).astype(jnp.bfloat16)
        wide = lax.dot_general(
            tall, repeat, (((1,), (1,)), ((), ())), preferred_element_type=jnp.float32
        )
        same = (
            lax.broadcasted_iota(jnp.int32, (total, total), 0) % rows
            == lax.broadcasted_iota(jnp.int32, (total, total), 1) % rows
        )
        matrix[...] = jnp.where(same, wide, 0.0).astype(jnp.bfloat16)

        def stack_one(place, block):
            stacked[place] = (
                jnp.dot(left[...], block, preferred_element_type=jnp.float32)
                .astype(jnp.bfloat16)
                .reshape(ORIENT * 2, rows, QUART)
            )

        def coefficients(where):
            for o in range(ORIENT):
                value = jnp.dot(
                    stacked[:, where, :, 2 * o].reshape(planes * here * rows, QUART),
                    right[o, 0],
                    preferred_element_type=jnp.float32,
                ) + jnp.dot(
                    stacked[:, where, :, 2 * o + 1].reshape(planes * here * rows, QUART),
                    right[o, 1],
                    preferred_element_type=jnp.float32,
                )
                value = value.astype(jnp.bfloat16).reshape(planes, here, rows, 2 * QUART)
                for p in range(planes):
                    coeffs[pl.ds((p * PLANE + where) * here, here), o] = value[p]

        own_rows = pl.ds(pl.multiple_of(plane * block + spot * rows, rows), window)
        core_rows = pl.ds(pl.multiple_of(core * rows, rows), window)

        def each(k, way, act):
            if k == 0:
                act(plane)
            elif way == 0:

                @pl.when(plane >= k)
                def _():
                    act(plane - k)

            else:

                @pl.when(plane + k < planes)
                def _():
                    act(plane + k)

        def arrive(k, n, way):
            def act(f):
                z_each(way == 0, f, n, lambda copy: copy.wait_recv(), True)
                z_each(way == 0, f, n, lambda copy: copy.start())
                spread_sideways(f, n)

            each(k, way, act)

        def stack_column(k, n, way):
            each(k, way, lambda f: stack_one((f, spot, n), column[f * here + n, own_rows, :]))

        def stack_sibling(k, n, way):
            def act(f):
                core_copy(f, n).wait_recv()
                stack_one((f, sibling, n), twin[0, f * here + n])

            each(k, way, act)

        def stack_across(k, n, way):
            def act(f):
                x_copy(f, n).wait_recv()
                pass_copy(f, n).start()
                stack_one((f, across, n), beside[f * here + n, core_rows, :])

            each(k, way, act)

        def stack_last(k, n, way):
            def act(f):
                pass_copy(f, n).wait_recv()
                stack_one((f, flip(across, 1), n), twin[1, f * here + n])

            each(k, way, act)

        events = [(0, n, 0) for n in range(here)] + [
            (k, n, way) for k in range(1, planes) for n in range(here) for way in range(2)
        ]
        late = LAG
        for i, event in enumerate(events):
            if event[0]:
                arrive(*event)
            stack_column(*event)
            if i >= 1:
                stack_sibling(*events[i - 1])
            if i >= late:
                stack_across(*events[i - late])
            if i >= late + 1:
                stack_last(*events[i - late - 1])
        stack_sibling(*events[-1])
        load_right.wait()
        coefficients(spot)
        coefficients(sibling)
        for event in events[len(events) - late :]:
            stack_across(*event)
        coefficients(across)
        for event in events[len(events) - late - 1 :]:
            stack_last(*event)
        coefficients(flip(across, 1))

        counts = [jnp.int32(0)] * NSEG
        for t in range(frames):
            for s in range(NSEG):
                counts[s] = counts[s] + jnp.where(segments[t] == s, 1, 0)
        picked, first = [], jnp.int32(0)
        for s in range(NSEG):
            rest = picks[s]
            for bit in reversed(range((PICK_LIMIT - 1).bit_length())):
                rest = jnp.where(rest >= counts[s] * (1 << bit), rest - counts[s] * (1 << bit), rest)
            picked.append(first + rest)
            first = first + counts[s]

        @pl.loop(0, frames)
        def _(t):
            ref = picked[NSEG - 1]
            for s in range(NSEG - 1):
                ref = jnp.where(segments[t] == s, picked[s], ref)
            ones = coeffs[t].astype(jnp.float32)
            base = coeffs[ref].astype(jnp.float32)
            real, imag = ones[..., :QUART], ones[..., QUART:]
            ref_real, ref_imag = base[..., :QUART], base[..., QUART:]
            prod_real = real * ref_real + imag * ref_imag
            prod_imag = imag * ref_real - real * ref_imag
            signal = prod_imag * lax.rsqrt(prod_real * prod_real + prod_imag * prod_imag + 1.0)
            phase[:, t] = signal.astype(jnp.bfloat16)
            denom[t] = jnp.sum(real * real + imag * imag, axis=0) + 1.0

        here_rows = pl.ds(pl.multiple_of(me * rows, rows), rows)

        def return_copy(j):
            to = peer(j)
            return pltpu.make_async_remote_copy(
                src_ref=moved.at[pl.ds(to * here, here)],
                dst_ref=out_hbm.at[:, here_rows, :],
                send_sem=send_b.at[j],
                recv_sem=recv_b.at[j],
                device_id={"frames": to},
            )

        crowd = parts // 2
        near = me // crowd

        def filter_half(number):
            span = pl.ds(number * (frames // 2), frames // 2)
            long_span = pl.ds(pl.multiple_of(number * (total // 2), total // 2), total // 2)
            for o in range(ORIENT):
                filtered = (
                    jnp.dot(
                        matrix[long_span, :],
                        phase[o].reshape(total, QUART),
                        preferred_element_type=jnp.float32,
                    )
                    .astype(jnp.bfloat16)
                    .astype(jnp.float32)
                    .reshape(frames // 2, rows, QUART)
                )
                real = coeffs[span, o, :, :QUART].astype(jnp.float32)
                imag = coeffs[span, o, :, QUART:].astype(jnp.float32)
                term = (real * real + imag * imag) * filtered
                if o == 0:
                    numer[...] = term
                elif o < ORIENT - 1:
                    numer[...] += term
                else:
                    moved[span] = ((numer[...] + term) / denom[span]).astype(jnp.bfloat16)

        filter_half(1 - near)

        @pl.loop(0, crowd)
        def _(k):
            to = (1 - near) * crowd + lax.rem(me + k, crowd)
            return_copy(lax.rem(to + parts - me, parts)).start()

        filter_half(near)

        @pl.loop(1, crowd)
        def _(k):
            to = near * crowd + lax.rem(me + k, crowd)
            return_copy(lax.rem(to + parts - me, parts)).start()

        store = pltpu.make_async_copy(
            moved.at[pl.ds(me * here, here)], out_hbm.at[:, here_rows, :], store_sem
        )
        store.start()

        for k, n, way in events:

            def sent(f):
                if k == 0 or way == 0:
                    z_each(True, f, n, lambda copy: copy.wait_send())
                if k == 0 or way == 1:
                    z_each(False, f, n, lambda copy: copy.wait_send())
                x_copy(f, n).wait_send()
                core_copy(f, n).wait_send()
                pass_copy(f, n).wait_send()

            each(k, way, sent)

        @pl.loop(1, parts)
        def _(j):
            return_copy(j).wait_recv()

        @pl.loop(1, parts)
        def _(j):
            return_copy(j).wait_send()

        store.wait()

    bf16, f32, dma = jnp.bfloat16, jnp.float32, pltpu.SemaphoreType.DMA
    anywhere = pl.BlockSpec(memory_space=pl.ANY)
    vmem = pl.BlockSpec(memory_space=pltpu.VMEM)
    smem = pl.BlockSpec(memory_space=pltpu.SMEM)
    return pl.pallas_call(
        kernel,
        out_shape=jax.ShapeDtypeStruct((here, QUART, QUART), bf16),
        in_specs=[smem, smem, vmem, anywhere, anywhere, anywhere, vmem, anywhere],
        out_specs=anywhere,
        scratch_shapes=[
            pltpu.VMEM((here, IMG, IMG), bf16),
            pltpu.VMEM((QUART, IMG), bf16),
            pltpu.VMEM((IMG, QUART), bf16),
            pltpu.VMEM((ORIENT, 2, QUART, 2 * QUART), bf16),
            pltpu.VMEM((here, IMG, QUART), bf16),
            pltpu.VMEM((planes * here, QUART + 2 * REACH, QUART), bf16),
            pltpu.VMEM((planes * here, pair_window, QUART), bf16),
            pltpu.VMEM((2, planes * here, window, QUART), bf16),
            pltpu.VMEM((planes, PLANE, here, ORIENT * 2, rows, QUART), bf16),
            pltpu.VMEM((frames, ORIENT, rows, 2 * QUART), bf16),
            pltpu.VMEM((ORIENT, frames, rows, QUART), bf16),
            pltpu.VMEM((total, total), bf16),
            pltpu.VMEM((frames // 2, rows, QUART), f32),
            pltpu.VMEM((frames, rows, QUART), f32),
            pltpu.VMEM((frames, rows, QUART), bf16),
            dma((3 + here * chunks,)),
            dma,
            dma((2, planes, here)),
            dma((2, planes, here)),
            dma((planes, here)),
            dma((planes, here)),
            dma((2, planes, here)),
            dma((2, planes, here)),
            dma((parts,)),
            dma((parts,)),
        ],
        compiler_params=pltpu.CompilerParams(
            collective_id=0, has_side_effects=True, vmem_limit_bytes=60 * 1024 * 1024
        ),
    )


def kernel_body(parts, video_frames, segments, ref_pick, band_taps):
    here = video_frames.shape[0]
    rows = QUART // parts
    down = down_table()
    return make_kernel(parts, here, rows)(
        segments,
        ref_pick,
        band_taps[None, :],
        video_frames,
        jnp.asarray(down),
        jnp.asarray(np.ascontiguousarray(down.T)),
        jnp.asarray(left_window(rows)),
        jnp.asarray(right_tables()),
    ).astype(jnp.float32)


def solution(mesh):
    parts = mesh.shape["frames"]
    if QUART % parts == 0 and (QUART // parts) % 16 == 0 and parts in (4, 8, 16):
        chosen = lambda *args: kernel_body(parts, *args)
    else:
        chosen = body
    in_specs = (P(("groups", "frames"), None, None), P("groups"), P("groups"), P())
    out_specs = P(("groups", "frames"), None, None)
    return jax.shard_map(chosen, mesh=mesh, in_specs=in_specs, out_specs=out_specs, check_vma=False)
```

```python
import math

import jax
import numpy as np
import jax.numpy as jnp
from jax import lax
from jax.experimental import pallas as pl
from jax.experimental.pallas import tpu as pltpu
from jax.sharding import PartitionSpec as P

IMG = 1024
ORIENT = 4
NSEG = 4
QUART = 256


blur_sigma = 2.0
gabor_sigma = 2.0
wave_number = math.pi / 2.0
gabor_gain = 2.0


def spread(x, axis, root):
    mine = lax.axis_index(axis) == root
    return lax.psum(jnp.where(mine, x, jnp.zeros_like(x)), axis)


def make_down(full_size, quarter):
    position = jnp.arange(quarter, dtype=jnp.float32)[:, None]
    columns = jnp.arange(full_size, dtype=jnp.float32)[None, :]
    offset_grid = columns - 4.0 * position - 1.5
    weight = jnp.exp(-offset_grid * offset_grid / (2.0 * blur_sigma * blur_sigma))
    return (weight / jnp.sum(weight, axis=1, keepdims=True)).astype(jnp.bfloat16)


def gabor_tables(quarter, orient):
    position = jnp.arange(quarter, dtype=jnp.float32)
    offset_grid = position[None, :] - position[:, None]
    envelope = gabor_gain * jnp.exp(-offset_grid * offset_grid / (2.0 * gabor_sigma * gabor_sigma))
    angles = jnp.arange(orient, dtype=jnp.float32) * (math.pi / orient)
    wave_x = wave_number * jnp.cos(angles)
    wave_y = wave_number * jnp.sin(angles)
    phase_y = wave_y[:, None, None] * offset_grid[None]
    left_table = jnp.stack([envelope * jnp.cos(phase_y), envelope * jnp.sin(phase_y)], axis=2)
    left_table = left_table.reshape(orient * quarter * 2, quarter).astype(jnp.bfloat16)
    phase_x = wave_x[:, None, None] * (-offset_grid)[None]
    real_part = envelope * jnp.cos(phase_x)
    imag_part = envelope * jnp.sin(phase_x)
    upper_half = jnp.concatenate([real_part, imag_part], axis=2)
    lower_half = jnp.concatenate([-imag_part, real_part], axis=2)
    right_table = jnp.concatenate([upper_half, lower_half], axis=1).astype(jnp.bfloat16)
    return (left_table, right_table)


def phase_terms(coeffs, per_frame):
    quarter = coeffs.shape[-1] // 2
    coeff_real = coeffs[..., :quarter].astype(jnp.float32)
    coeff_imag = coeffs[..., quarter:].astype(jnp.float32)
    ref_real = per_frame[..., :quarter].astype(jnp.float32)
    ref_imag = per_frame[..., quarter:].astype(jnp.float32)
    prod_real = coeff_real * ref_real + coeff_imag * ref_imag
    prod_imag = coeff_imag * ref_real - coeff_real * ref_imag
    phase_signal = (
        prod_imag / jnp.sqrt(prod_real * prod_real + prod_imag * prod_imag + 1.0)
    ).astype(jnp.bfloat16)
    amplitude = coeff_real * coeff_real + coeff_imag * coeff_imag
    return (phase_signal, amplitude)


def taps_matrix(band_taps, frame_count):
    frame_index = jnp.arange(frame_count, dtype=jnp.int32)
    lag_grid = frame_index[:, None] - frame_index[None, :]
    one_hot = (
        lag_grid[:, :, None] == jnp.arange(band_taps.shape[0], dtype=jnp.int32)[None, None, :]
    ).astype(jnp.float32)
    return jnp.einsum("tsk,k->ts", one_hot, band_taps.astype(jnp.float32)).astype(jnp.bfloat16)


def segment_refs(segments, ref_pick, segment_count):
    numbers = jnp.arange(segment_count, dtype=jnp.int32)
    starts = jnp.sum((segments[None, :] < numbers[:, None]).astype(jnp.int32), axis=1)
    counts = jnp.sum((segments[None, :] == numbers[:, None]).astype(jnp.int32), axis=1)
    return starts + ref_pick % counts


def body(video_frames, segments, ref_pick, band_taps):
    frames_here = video_frames.shape[0]
    down_matrix = make_down(IMG, QUART)
    left_table, right_table = gabor_tables(QUART, ORIENT)

    def reduce_frames(pictures):
        half_done = jnp.einsum(
            "nia,qa->niq", pictures, down_matrix, preferred_element_type=jnp.float32
        ).astype(jnp.bfloat16)
        return jnp.einsum(
            "qi,nik->nqk", down_matrix, half_done, preferred_element_type=jnp.float32
        ).astype(jnp.bfloat16)

    def filter_frames(reduced):
        stacked = jnp.einsum(
            "ra,nak->nrk", left_table, reduced, preferred_element_type=jnp.float32
        ).astype(jnp.bfloat16)
        stacked = stacked.reshape(reduced.shape[0], ORIENT, QUART, 2 * QUART)
        return jnp.einsum(
            "noya,oab->noyb", stacked, right_table, preferred_element_type=jnp.float32
        ).astype(jnp.bfloat16)

    small_own = reduce_frames(video_frames)
    coeff_own = filter_frames(small_own)
    ref_frames = segment_refs(segments, ref_pick, NSEG)
    gathered = []
    for segment in range(NSEG):
        root_index = ref_frames[segment] // frames_here
        local_index = ref_frames[segment] % frames_here
        payload = lax.dynamic_index_in_dim(video_frames, local_index, 0, keepdims=False)
        gathered.append(spread(payload, "frames", root_index))
    ref_coeff = filter_frames(reduce_frames(jnp.stack(gathered)))
    first_frame = lax.axis_index("frames") * frames_here
    own_ids = lax.dynamic_slice_in_dim(segments, first_frame, frames_here)
    select = (own_ids[:, None] == jnp.arange(NSEG, dtype=jnp.int32)[None, :]).astype(jnp.bfloat16)
    per_frame = jnp.dot(select, ref_coeff.reshape(NSEG, -1), preferred_element_type=jnp.float32)
    per_frame = per_frame.astype(jnp.bfloat16).reshape(coeff_own.shape)
    phase_signal, amplitude = phase_terms(coeff_own, per_frame)
    phase_signal = phase_signal.reshape(frames_here, ORIENT, QUART * QUART)
    pixel_rows = lax.all_to_all(phase_signal, "frames", split_axis=2, concat_axis=0, tiled=True)
    matrix = taps_matrix(band_taps, pixel_rows.shape[0])
    filtered = jnp.einsum(
        "ts,sop->top", matrix, pixel_rows, preferred_element_type=jnp.float32
    ).astype(jnp.bfloat16)
    filtered = lax.all_to_all(filtered, "frames", split_axis=0, concat_axis=2, tiled=True)
    filtered = filtered.reshape(frames_here, ORIENT, QUART, QUART).astype(jnp.float32)
    return jnp.sum(amplitude * filtered, axis=1) / (jnp.sum(amplitude, axis=1) + 1.0)


PICK_LIMIT = 4096
REACH = 32


def down_table():
    position = np.arange(QUART, dtype=np.float32)[:, None]
    columns = np.arange(IMG, dtype=np.float32)[None, :]
    offset = columns - np.float32(4.0) * position - np.float32(1.5)
    weight = np.exp(-offset * offset / np.float32(2.0 * blur_sigma * blur_sigma))
    return (weight / np.sum(weight, axis=1, keepdims=True)).astype(jnp.bfloat16)


def waves():
    angles = np.arange(ORIENT, dtype=np.float32) * np.float32(math.pi / ORIENT)
    return np.float32(wave_number) * np.cos(angles), np.float32(wave_number) * np.sin(angles)


def gabor_envelope(offset):
    return np.float32(gabor_gain) * np.exp(-offset * offset / np.float32(2.0 * gabor_sigma * gabor_sigma))


def left_window(rows):
    offset = (
        np.arange(rows + 2 * REACH, dtype=np.float32)[None, :]
        - REACH
        - np.arange(rows, dtype=np.float32)[:, None]
    )
    envelope = gabor_envelope(offset)
    phase = waves()[1][:, None, None] * offset[None]
    table = np.stack([envelope * np.cos(phase), envelope * np.sin(phase)], axis=1)
    return table.reshape(ORIENT * 2 * rows, -1).astype(jnp.bfloat16)


def right_tables():
    position = np.arange(QUART, dtype=np.float32)
    offset = position[:, None] - position[None, :]
    envelope = gabor_envelope(offset)
    phase = waves()[0][:, None, None] * offset[None]
    real, imag = envelope * np.cos(phase), envelope * np.sin(phase)
    return np.stack([real, imag], axis=1).astype(jnp.bfloat16)


PLANE = 4
PAIR = 2
LAG = 3
STRIP = 128
UNROLL = 2
ORDERS = ((0, 1, 2), (0, 1, 2))


def flip(number, bits):
    step = 1
    while step <= bits:
        if bits & step:
            number = number + step - 2 * step * ((number // step) % 2)
        step *= 2
    return number


def make_kernel(parts, here, rows):
    frames = parts * here
    planes = parts // PLANE
    window = rows + 2 * REACH
    pair_window = PAIR * rows + 2 * REACH
    total = frames * rows
    chunks = 2
    strips = QUART // STRIP

    def kernel(
        segments, picks, taps, video_hbm, down_hbm, left, right_hbm, out_hbm,
        video, down, right, half, column, beside, twin, stacked, coeffs,
        powers, phase, matrix, denom, moved,
        load_sem, store_sem, send_z, recv_z, send_x, recv_x, send_c, recv_c, send_b, recv_b,
    ):
        me = lax.axis_index("frames")
        plane, spot = me // PLANE, me % PLANE
        across, sibling = flip(spot, PAIR), flip(spot, 1)
        side, core = spot // PAIR, spot % PAIR
        barrier = pltpu.get_barrier_semaphore()

        def peer(j):
            return lax.rem(me + j, parts)

        def piece(n, part):
            height = IMG // chunks
            where = pl.ds(part * height, height)
            return pltpu.make_async_copy(
                video_hbm.at[n, where], video.at[n, where], load_sem.at[3 + n * chunks + part]
            )

        load_down = pltpu.make_async_copy(down_hbm, down, load_sem.at[1])
        load_right = pltpu.make_async_copy(right_hbm, right, load_sem.at[2])
        load_down.start()
        for n in range(here):
            for part in range(chunks):
                piece(n, part).start()
        load_right.start()

        def greet(where):
            pl.semaphore_signal(barrier, inc=1, device_id={"frames": where})

        others = [flip(plane, j) for j in range(1, planes)]
        for to in reversed(others):
            greet(to * PLANE + spot)
        greet(plane * PLANE + across)
        greet(plane * PLANE + sibling)

        blank = jnp.zeros((planes * here, REACH, QUART), jnp.bfloat16)
        column[:, :REACH, :] = blank
        column[:, REACH + QUART :, :] = blank

        block = PLANE * rows
        low, high = REACH, REACH + QUART

        def z_copy(f, n, q):
            part = column.at[f * here + n, max(block * q, low) : min(block * (q + 2), high), :]
            return pltpu.make_async_remote_copy(
                src_ref=part,
                dst_ref=part,
                send_sem=send_z.at[q, n],
                recv_sem=recv_z.at[f, n],
                device_id={"frames": q * PLANE + spot},
            )

        def z_part(f, n, to, act):
            for q in range(planes):

                @pl.when(to == q)
                def _():
                    act(z_copy(f, n, q))

        def z_send(n, to):
            z_part(plane, n, to, lambda copy: copy.start())

        def x_copy(f, n):
            first = pl.multiple_of(plane * block + (1 - side) * PAIR * rows, rows)
            return pltpu.make_async_remote_copy(
                src_ref=column.at[f * here + n, pl.ds(first, pair_window), :],
                dst_ref=beside.at[f * here + n],
                send_sem=send_x.at[f, n],
                recv_sem=recv_x.at[f, n],
                device_id={"frames": plane * PLANE + across},
            )

        def core_copy(f, n):
            first = pl.multiple_of(plane * block + sibling * rows, rows)
            return pltpu.make_async_remote_copy(
                src_ref=column.at[f * here + n, pl.ds(first, window), :],
                dst_ref=twin.at[0, f * here + n],
                send_sem=send_c.at[0, f, n],
                recv_sem=recv_c.at[0, f, n],
                device_id={"frames": plane * PLANE + sibling},
            )

        def pass_copy(f, n):
            first = pl.multiple_of((1 - core) * rows, rows)
            return pltpu.make_async_remote_copy(
                src_ref=beside.at[f * here + n, pl.ds(first, window), :],
                dst_ref=twin.at[1, f * here + n],
                send_sem=send_c.at[1, f, n],
                recv_sem=recv_c.at[1, f, n],
                device_id={"frames": plane * PLANE + sibling},
            )

        def spread_sideways(f, n):
            x_copy(f, n).start()
            core_copy(f, n).start()

        load_down.wait()
        for n in range(here):
            for part in range(chunks):
                piece(n, part).wait()
                where = slice(part * (IMG // chunks), (part + 1) * (IMG // chunks))
                half[n, where] = lax.dot_general(
                    video[n, where], down[...], (((1,), (1,)), ((), ())),
                    preferred_element_type=jnp.float32,
                ).astype(jnp.bfloat16)
            column[plane * here + n, REACH : REACH + QUART, :] = jnp.dot(
                down[...], half[n], preferred_element_type=jnp.float32
            ).astype(jnp.bfloat16)
            if n == 0:
                pl.semaphore_wait(barrier, planes + 1)
            spread_sideways(plane, n)
            for i in ORDERS[min(n, 1)]:
                if i < planes - 1:
                    z_send(n, others[i])

        lag = lax.broadcasted_iota(jnp.int32, (frames, frames), 0) - lax.broadcasted_iota(
            jnp.int32, (frames, frames), 1
        )
        toeplitz = jnp.zeros((frames, frames), jnp.float32)
        tap_row = taps[...].astype(jnp.float32)
        for k in range(min(taps.shape[1], frames)):
            toeplitz = jnp.where(lag == k, tap_row[:, k : k + 1], toeplitz)
        owner = lax.broadcasted_iota(jnp.int32, (total, frames), 0) // rows
        repeat = jnp.where(
            owner == lax.broadcasted_iota(jnp.int32, (total, frames), 1), 1.0, 0.0
        ).astype(jnp.bfloat16)
        tall = jnp.dot(
            repeat, toeplitz.astype(jnp.bfloat16), preferred_element_type=jnp.float32
        ).astype(jnp.bfloat16)
        wide = lax.dot_general(
            tall, repeat, (((1,), (1,)), ((), ())), preferred_element_type=jnp.float32
        )
        same = (
            lax.broadcasted_iota(jnp.int32, (total, total), 0) % rows
            == lax.broadcasted_iota(jnp.int32, (total, total), 1) % rows
        )
        matrix[...] = jnp.where(same, wide, 0.0).astype(jnp.bfloat16)

        def stack_one(place, block):
            stacked[place] = (
                jnp.dot(left[...], block, preferred_element_type=jnp.float32)
                .astype(jnp.bfloat16)
                .reshape(ORIENT * 2, rows, QUART)
            )

        def coefficients(where):
            tall_rows = planes * here * rows
            total_power = [0.0] * strips
            for o in range(ORIENT):
                even = stacked[:, where, :, 2 * o].reshape(tall_rows, QUART)
                odd = stacked[:, where, :, 2 * o + 1].reshape(tall_rows, QUART)

                def times(left_part, which):
                    return jnp.dot(left_part, right[o, which], preferred_element_type=jnp.float32)

                real = (times(even, 0) - times(odd, 1)).astype(jnp.bfloat16)
                imag = (times(even, 1) + times(odd, 0)).astype(jnp.bfloat16)
                wide_real, wide_imag = real.astype(jnp.float32), imag.astype(jnp.float32)
                power = wide_real * wide_real + wide_imag * wide_imag
                slot = slice(o % 2 * STRIP, (o % 2 + 1) * STRIP)
                imag_slot = slice(QUART + o % 2 * STRIP, QUART + (o % 2 + 1) * STRIP)
                for h in range(strips):
                    columns = slice(h * STRIP, (h + 1) * STRIP)
                    total_power[h] = total_power[h] + power[:, columns]

                    def split(value):
                        return value[:, columns].reshape(planes, here, rows, STRIP)

                    for p in range(planes):
                        at = pl.ds((p * PLANE + where) * here, here)
                        coeffs[h, at, o // 2, :, slot] = split(real)[p]
                        coeffs[h, at, o // 2, :, imag_slot] = split(imag)[p]
                        powers[h, at, o // 2, :, slot] = split(power)[p]
            for h in range(strips):
                whole = (total_power[h] + 1.0).reshape(planes, here, rows, STRIP)
                for p in range(planes):
                    denom[h, pl.ds((p * PLANE + where) * here, here)] = whole[p]

        own_rows = pl.ds(pl.multiple_of(plane * block + spot * rows, rows), window)
        core_rows = pl.ds(pl.multiple_of(core * rows, rows), window)

        def arrive(f, n):
            z_part(f, n, plane, lambda copy: copy.wait_recv())
            spread_sideways(f, n)

        def stack_column(f, n):
            stack_one((f, spot, n), column[f * here + n, own_rows, :])

        def stack_sibling(f, n):
            core_copy(f, n).wait_recv()
            stack_one((f, sibling, n), twin[0, f * here + n])

        def stack_across(f, n):
            x_copy(f, n).wait_recv()
            pass_copy(f, n).start()
            stack_one((f, across, n), beside[f * here + n, core_rows, :])

        def stack_last(f, n):
            pass_copy(f, n).wait_recv()
            stack_one((f, flip(across, 1), n), twin[1, f * here + n])

        events = [(plane, n) for n in range(here)] + [
            (others[i], n)
            for n in range(here)
            for i in ORDERS[min(n, 1)]
            if i < planes - 1
        ]
        late = LAG
        for i, event in enumerate(events):
            if i >= here:
                arrive(*event)
            stack_column(*event)
            if i >= 1:
                stack_sibling(*events[i - 1])
            if i >= late:
                stack_across(*events[i - late])
            if i >= late + 1:
                stack_last(*events[i - late - 1])
        stack_sibling(*events[-1])
        load_right.wait()
        coefficients(spot)
        coefficients(sibling)
        for event in events[max(len(events) - late, 0) :]:
            stack_across(*event)
        coefficients(across)
        for event in events[max(len(events) - late - 1, 0) :]:
            stack_last(*event)
        coefficients(flip(across, 1))

        counts = [jnp.int32(0)] * NSEG
        for t in range(frames):
            for s in range(NSEG):
                counts[s] = counts[s] + jnp.where(segments[t] == s, 1, 0)
        picked, first = [], jnp.int32(0)
        for s in range(NSEG):
            rest = picks[s]
            for bit in reversed(range((PICK_LIMIT - 1).bit_length())):
                rest = jnp.where(rest >= counts[s] * (1 << bit), rest - counts[s] * (1 << bit), rest)
            picked.append(first + rest)
            first = first + counts[s]

        here_rows = pl.ds(pl.multiple_of(me * rows, rows), rows)

        def phases(h):
            @pl.loop(0, frames // UNROLL)
            def _(step):
                for u in range(UNROLL):
                    t = step * UNROLL + u
                    ref = picked[NSEG - 1]
                    for s in range(NSEG - 1):
                        ref = jnp.where(segments[t] == s, picked[s], ref)
                    ones = coeffs[h, t].astype(jnp.float32)
                    base = coeffs[h, ref].astype(jnp.float32)
                    prod_imag = ones[..., QUART:] * base[..., :QUART] - ones[..., :QUART] * base[..., QUART:]
                    signal = prod_imag * lax.rsqrt(powers[h, t] * powers[h, ref] + 1.0)
                    phase[:, t] = signal.astype(jnp.bfloat16)

        def return_copy(h, j):
            to = peer(j)
            return pltpu.make_async_remote_copy(
                src_ref=moved.at[h, pl.ds(to * here, here)],
                dst_ref=out_hbm.at[:, here_rows, h * STRIP : (h + 1) * STRIP],
                send_sem=send_b.at[h, j],
                recv_sem=recv_b.at[h, j],
                device_id={"frames": to},
            )

        def store(h):
            return pltpu.make_async_copy(
                moved.at[h, pl.ds(me * here, here)],
                out_hbm.at[:, here_rows, h * STRIP : (h + 1) * STRIP],
                store_sem.at[h],
            )

        crowd = parts // 2
        near = me // crowd

        def filter_half(h, number):
            span = slice(number * (frames // 2), (number + 1) * (frames // 2))
            until = (number + 1) * (total // 2)
            numer = 0.0
            for q in range(ORIENT // 2):
                filtered = (
                    jnp.dot(
                        matrix[number * (total // 2) : until, :until],
                        phase[q].reshape(total, QUART)[:until],
                        preferred_element_type=jnp.float32,
                    )
                    .astype(jnp.bfloat16)
                    .astype(jnp.float32)
                    .reshape(frames // 2, rows, QUART)
                )
                numer = numer + powers[h, span, q] * filtered
            numer = numer[..., :STRIP] + numer[..., STRIP:]
            moved[h, span] = (numer / denom[h, span]).astype(jnp.bfloat16)

        for h in range(strips):
            phases(h)
            for close in (False, True):
                for number in range(2):

                    @pl.when((near == number) == close)
                    def _():
                        filter_half(h, number)

                base_to = (near if close else 1 - near) * crowd

                @pl.loop(1 if close else 0, crowd)
                def _(k):
                    to = base_to + lax.rem(me + k, crowd)
                    return_copy(h, lax.rem(to + parts - me, parts)).start()

            store(h).start()

        for f, n in events:
            x_copy(f, n).wait_send()
            core_copy(f, n).wait_send()
            pass_copy(f, n).wait_send()
        for n in range(here):
            for to in others:
                z_part(plane, n, to, lambda copy: copy.wait_send())

        for h in range(strips):

            @pl.loop(1, parts)
            def _(j):
                return_copy(h, j).wait_recv()
                return_copy(h, j).wait_send()

            store(h).wait()

    bf16, f32, dma = jnp.bfloat16, jnp.float32, pltpu.SemaphoreType.DMA
    anywhere = pl.BlockSpec(memory_space=pl.ANY)
    vmem = pl.BlockSpec(memory_space=pltpu.VMEM)
    smem = pl.BlockSpec(memory_space=pltpu.SMEM)
    return pl.pallas_call(
        kernel,
        out_shape=jax.ShapeDtypeStruct((here, QUART, QUART), bf16),
        in_specs=[smem, smem, vmem, anywhere, anywhere, vmem, anywhere],
        out_specs=anywhere,
        scratch_shapes=[
            pltpu.VMEM((here, IMG, IMG), bf16),
            pltpu.VMEM((QUART, IMG), bf16),
            pltpu.VMEM((ORIENT, 2, QUART, QUART), bf16),
            pltpu.VMEM((here, IMG, QUART), bf16),
            pltpu.VMEM((planes * here, QUART + 2 * REACH, QUART), bf16),
            pltpu.VMEM((planes * here, pair_window, QUART), bf16),
            pltpu.VMEM((2, planes * here, window, QUART), bf16),
            pltpu.VMEM((planes, PLANE, here, ORIENT * 2, rows, QUART), bf16),
            pltpu.VMEM((strips, frames, ORIENT // 2, rows, 2 * QUART), bf16),
            pltpu.VMEM((strips, frames, ORIENT // 2, rows, QUART), f32),
            pltpu.VMEM((ORIENT // 2, frames, rows, QUART), bf16),
            pltpu.VMEM((total, total), bf16),
            pltpu.VMEM((strips, frames, rows, STRIP), f32),
            pltpu.VMEM((strips, frames, rows, STRIP), bf16),
            dma((3 + here * chunks,)),
            dma((strips,)),
            dma((planes, here)),
            dma((planes, here)),
            dma((planes, here)),
            dma((planes, here)),
            dma((2, planes, here)),
            dma((2, planes, here)),
            dma((strips, parts)),
            dma((strips, parts)),
        ],
        compiler_params=pltpu.CompilerParams(
            collective_id=0, has_side_effects=True, vmem_limit_bytes=60 * 1024 * 1024
        ),
    )


def kernel_body(parts, video_frames, segments, ref_pick, band_taps):
    here = video_frames.shape[0]
    rows = QUART // parts
    down = down_table()
    return make_kernel(parts, here, rows)(
        segments,
        ref_pick,
        band_taps[None, :],
        video_frames,
        jnp.asarray(down),
        jnp.asarray(left_window(rows)),
        jnp.asarray(right_tables()),
    ).astype(jnp.float32)


def solution(mesh):
    parts = mesh.shape["frames"]
    if QUART % parts == 0 and (QUART // parts) % 16 == 0 and parts in (4, 8, 16):
        chosen = lambda *args: kernel_body(parts, *args)
    else:
        chosen = body
    in_specs = (P(("groups", "frames"), None, None), P("groups"), P("groups"), P())
    out_specs = P(("groups", "frames"), None, None)
    return jax.shard_map(chosen, mesh=mesh, in_specs=in_specs, out_specs=out_specs, check_vma=False)
```

```python
import math

import jax
import numpy as np
import jax.numpy as jnp
from jax import lax
from jax.experimental import pallas as pl
from jax.experimental.pallas import tpu as pltpu
from jax.sharding import PartitionSpec as P

IMG = 1024
ORIENT = 4
NSEG = 4
QUART = 256


blur_sigma = 2.0
gabor_sigma = 2.0
wave_number = math.pi / 2.0
gabor_gain = 2.0


def spread(x, axis, root):
    mine = lax.axis_index(axis) == root
    return lax.psum(jnp.where(mine, x, jnp.zeros_like(x)), axis)


def make_down(full_size, quarter):
    position = jnp.arange(quarter, dtype=jnp.float32)[:, None]
    columns = jnp.arange(full_size, dtype=jnp.float32)[None, :]
    offset_grid = columns - 4.0 * position - 1.5
    weight = jnp.exp(-offset_grid * offset_grid / (2.0 * blur_sigma * blur_sigma))
    return (weight / jnp.sum(weight, axis=1, keepdims=True)).astype(jnp.bfloat16)


def gabor_tables(quarter, orient):
    position = jnp.arange(quarter, dtype=jnp.float32)
    offset_grid = position[None, :] - position[:, None]
    envelope = gabor_gain * jnp.exp(-offset_grid * offset_grid / (2.0 * gabor_sigma * gabor_sigma))
    angles = jnp.arange(orient, dtype=jnp.float32) * (math.pi / orient)
    wave_x = wave_number * jnp.cos(angles)
    wave_y = wave_number * jnp.sin(angles)
    phase_y = wave_y[:, None, None] * offset_grid[None]
    left_table = jnp.stack([envelope * jnp.cos(phase_y), envelope * jnp.sin(phase_y)], axis=2)
    left_table = left_table.reshape(orient * quarter * 2, quarter).astype(jnp.bfloat16)
    phase_x = wave_x[:, None, None] * (-offset_grid)[None]
    real_part = envelope * jnp.cos(phase_x)
    imag_part = envelope * jnp.sin(phase_x)
    upper_half = jnp.concatenate([real_part, imag_part], axis=2)
    lower_half = jnp.concatenate([-imag_part, real_part], axis=2)
    right_table = jnp.concatenate([upper_half, lower_half], axis=1).astype(jnp.bfloat16)
    return (left_table, right_table)


def phase_terms(coeffs, per_frame):
    quarter = coeffs.shape[-1] // 2
    coeff_real = coeffs[..., :quarter].astype(jnp.float32)
    coeff_imag = coeffs[..., quarter:].astype(jnp.float32)
    ref_real = per_frame[..., :quarter].astype(jnp.float32)
    ref_imag = per_frame[..., quarter:].astype(jnp.float32)
    prod_real = coeff_real * ref_real + coeff_imag * ref_imag
    prod_imag = coeff_imag * ref_real - coeff_real * ref_imag
    phase_signal = (
        prod_imag / jnp.sqrt(prod_real * prod_real + prod_imag * prod_imag + 1.0)
    ).astype(jnp.bfloat16)
    amplitude = coeff_real * coeff_real + coeff_imag * coeff_imag
    return (phase_signal, amplitude)


def taps_matrix(band_taps, frame_count):
    frame_index = jnp.arange(frame_count, dtype=jnp.int32)
    lag_grid = frame_index[:, None] - frame_index[None, :]
    one_hot = (
        lag_grid[:, :, None] == jnp.arange(band_taps.shape[0], dtype=jnp.int32)[None, None, :]
    ).astype(jnp.float32)
    return jnp.einsum("tsk,k->ts", one_hot, band_taps.astype(jnp.float32)).astype(jnp.bfloat16)


def segment_refs(segments, ref_pick, segment_count):
    numbers = jnp.arange(segment_count, dtype=jnp.int32)
    starts = jnp.sum((segments[None, :] < numbers[:, None]).astype(jnp.int32), axis=1)
    counts = jnp.sum((segments[None, :] == numbers[:, None]).astype(jnp.int32), axis=1)
    return starts + ref_pick % counts


def body(video_frames, segments, ref_pick, band_taps):
    frames_here = video_frames.shape[0]
    down_matrix = make_down(IMG, QUART)
    left_table, right_table = gabor_tables(QUART, ORIENT)

    def reduce_frames(pictures):
        half_done = jnp.einsum(
            "nia,qa->niq", pictures, down_matrix, preferred_element_type=jnp.float32
        ).astype(jnp.bfloat16)
        return jnp.einsum(
            "qi,nik->nqk", down_matrix, half_done, preferred_element_type=jnp.float32
        ).astype(jnp.bfloat16)

    def filter_frames(reduced):
        stacked = jnp.einsum(
            "ra,nak->nrk", left_table, reduced, preferred_element_type=jnp.float32
        ).astype(jnp.bfloat16)
        stacked = stacked.reshape(reduced.shape[0], ORIENT, QUART, 2 * QUART)
        return jnp.einsum(
            "noya,oab->noyb", stacked, right_table, preferred_element_type=jnp.float32
        ).astype(jnp.bfloat16)

    small_own = reduce_frames(video_frames)
    coeff_own = filter_frames(small_own)
    ref_frames = segment_refs(segments, ref_pick, NSEG)
    gathered = []
    for segment in range(NSEG):
        root_index = ref_frames[segment] // frames_here
        local_index = ref_frames[segment] % frames_here
        payload = lax.dynamic_index_in_dim(video_frames, local_index, 0, keepdims=False)
        gathered.append(spread(payload, "frames", root_index))
    ref_coeff = filter_frames(reduce_frames(jnp.stack(gathered)))
    first_frame = lax.axis_index("frames") * frames_here
    own_ids = lax.dynamic_slice_in_dim(segments, first_frame, frames_here)
    select = (own_ids[:, None] == jnp.arange(NSEG, dtype=jnp.int32)[None, :]).astype(jnp.bfloat16)
    per_frame = jnp.dot(select, ref_coeff.reshape(NSEG, -1), preferred_element_type=jnp.float32)
    per_frame = per_frame.astype(jnp.bfloat16).reshape(coeff_own.shape)
    phase_signal, amplitude = phase_terms(coeff_own, per_frame)
    phase_signal = phase_signal.reshape(frames_here, ORIENT, QUART * QUART)
    pixel_rows = lax.all_to_all(phase_signal, "frames", split_axis=2, concat_axis=0, tiled=True)
    matrix = taps_matrix(band_taps, pixel_rows.shape[0])
    filtered = jnp.einsum(
        "ts,sop->top", matrix, pixel_rows, preferred_element_type=jnp.float32
    ).astype(jnp.bfloat16)
    filtered = lax.all_to_all(filtered, "frames", split_axis=0, concat_axis=2, tiled=True)
    filtered = filtered.reshape(frames_here, ORIENT, QUART, QUART).astype(jnp.float32)
    return jnp.sum(amplitude * filtered, axis=1) / (jnp.sum(amplitude, axis=1) + 1.0)


PICK_LIMIT = 4096
REACH = 32


def down_table():
    position = np.arange(QUART, dtype=np.float32)[:, None]
    columns = np.arange(IMG, dtype=np.float32)[None, :]
    offset = columns - np.float32(4.0) * position - np.float32(1.5)
    weight = np.exp(-offset * offset / np.float32(2.0 * blur_sigma * blur_sigma))
    return (weight / np.sum(weight, axis=1, keepdims=True)).astype(jnp.bfloat16)


def waves():
    angles = np.arange(ORIENT, dtype=np.float32) * np.float32(math.pi / ORIENT)
    return np.float32(wave_number) * np.cos(angles), np.float32(wave_number) * np.sin(angles)


def gabor_envelope(offset):
    return np.float32(gabor_gain) * np.exp(-offset * offset / np.float32(2.0 * gabor_sigma * gabor_sigma))


def left_window(rows):
    offset = (
        np.arange(rows + 2 * REACH, dtype=np.float32)[None, :]
        - REACH
        - np.arange(rows, dtype=np.float32)[:, None]
    )
    envelope = gabor_envelope(offset)
    phase = waves()[1][:, None, None] * offset[None]
    table = np.stack([envelope * np.cos(phase), envelope * np.sin(phase)], axis=1)
    return table.reshape(ORIENT * 2 * rows, -1).astype(jnp.bfloat16)


def right_tables():
    position = np.arange(QUART, dtype=np.float32)
    offset = position[:, None] - position[None, :]
    envelope = gabor_envelope(offset)
    phase = waves()[0][:, None, None] * offset[None]
    real, imag = envelope * np.cos(phase), envelope * np.sin(phase)
    return np.stack([real, imag], axis=1).astype(jnp.bfloat16)


PLANE = 4
PAIR = 2
LAG = 4
DUE = 3
STRIP = 128
UNROLL = 4
ORDERS = ((0, 1, 2), (0, 1, 2))


def flip(number, bits):
    step = 1
    while step <= bits:
        if bits & step:
            number = number + step - 2 * step * ((number // step) % 2)
        step *= 2
    return number


def make_kernel(parts, here, rows):
    frames = parts * here
    planes = parts // PLANE
    window = rows + 2 * REACH
    pair_window = PAIR * rows + 2 * REACH
    total = frames * rows
    chunks = 2
    strips = QUART // STRIP

    def kernel(
        segments, picks, taps, video_hbm, down_hbm, down_t_hbm, left, right_hbm, out_hbm,
        video, down, down_t, right, half, column, beside, twin, stacked, coeffs,
        powers, phase, matrix, denom, moved,
        load_sem, store_sem, send_z, recv_z, send_l, recv_l, send_x, recv_x, send_c, recv_c, send_b, recv_b,
    ):
        me = lax.axis_index("frames")
        plane, spot = me // PLANE, me % PLANE
        across, sibling = flip(spot, PAIR), flip(spot, 1)
        side, core = spot // PAIR, spot % PAIR
        barrier = pltpu.get_barrier_semaphore()

        def peer(j):
            return lax.rem(me + j, parts)

        def piece(n, part):
            height = IMG // chunks
            where = pl.ds(part * height, height)
            return pltpu.make_async_copy(
                video_hbm.at[n, where], video.at[n, where], load_sem.at[3 + n * chunks + part]
            )

        load_down = pltpu.make_async_copy(down_hbm, down, load_sem.at[1])
        load_down_t = pltpu.make_async_copy(down_t_hbm, down_t, load_sem.at[0])
        load_right = pltpu.make_async_copy(right_hbm, right, load_sem.at[2])
        load_down_t.start()
        for n in range(here):
            for part in range(chunks):
                piece(n, part).start()
            if n == 0:
                load_down.start()
        load_right.start()

        def greet(where):
            pl.semaphore_signal(barrier, inc=1, device_id={"frames": where})

        others = [flip(plane, j) for j in range(1, planes)]
        for to in reversed(others):
            greet(to * PLANE + spot)
        greet(plane * PLANE + across)
        greet(plane * PLANE + sibling)

        blank = jnp.zeros((planes * here, REACH, QUART), jnp.bfloat16)
        column[:, :REACH, :] = blank
        column[:, REACH + QUART :, :] = blank

        block = PLANE * rows
        low, high = REACH, REACH + QUART

        def early(q):
            return 0 if q < max(planes // 2, 1) else 1

        ahead = side == jnp.where(plane < max(planes // 2, 1), 0, 1)

        def bounds(first, last):
            return max(first, low), min(last, high)

        def early_rows(q):
            first = block * q + (PAIR * rows if early(q) else 0)
            return bounds(first, first + pair_window)

        def late_rows(q):
            first = block * q + (0 if early(q) else pair_window)
            return bounds(first, first + PAIR * rows)

        def z_copy(f, n, q):
            first, last = early_rows(q)
            part = column.at[f * here + n, first:last, :]
            return pltpu.make_async_remote_copy(
                src_ref=part,
                dst_ref=part,
                send_sem=send_z.at[q, n],
                recv_sem=recv_z.at[f, n],
                device_id={"frames": q * PLANE + spot},
            )

        def z_part(f, n, to, act):
            for q in range(planes):

                @pl.when(to == q)
                def _():
                    act(z_copy(f, n, q))

        def z_send(n, to):
            z_part(plane, n, to, lambda copy: copy.start())

        def late_copy(f, n, q, straight):
            first, last = late_rows(q)
            inside = 0 if early(q) else pair_window - PAIR * rows
            inside = inside + first - (block * q + (0 if early(q) else pair_window))
            target = (
                column.at[f * here + n, first:last, :]
                if straight
                else beside.at[f * here + n, inside : inside + last - first, :]
            )
            other_side = 1 - early(q)
            return pltpu.make_async_remote_copy(
                src_ref=column.at[f * here + n, first:last, :],
                dst_ref=target,
                send_sem=send_l.at[q, n],
                recv_sem=recv_l.at[0 if straight else 1, f, n],
                device_id={"frames": q * PLANE + other_side * PAIR + core},
            )

        def has_late(q):
            first, last = late_rows(q)
            return last > first

        def late_own(n, act):
            for q in range(planes):
                if has_late(q):

                    @pl.when((side == 1 - early(q)) & (plane != q))
                    def _():
                        act(late_copy(plane, n, q, True))

                    @pl.when(side == early(q))
                    def _():
                        act(late_copy(plane, n, q, False))

        def late_wait(f, n, straight):
            for q in range(planes):
                if has_late(q):

                    @pl.when(plane == q)
                    def _():
                        late_copy(f, n, q, straight).wait_recv()

        def x_copy(f, n, q, whole):
            first = block * q + (PAIR * rows if early(q) else 0)
            inside, size = 0, pair_window
            if not whole:
                first, size = block * q + PAIR * rows, pair_window - PAIR * rows
                inside = PAIR * rows if early(q) else 0
            return pltpu.make_async_remote_copy(
                src_ref=column.at[f * here + n, first : first + size, :],
                dst_ref=beside.at[f * here + n, inside : inside + size, :],
                send_sem=send_x.at[f, n],
                recv_sem=recv_x.at[f, n],
                device_id={"frames": plane * PLANE + across},
            )

        def x_each(f, n, to_ahead, act):
            for q in range(planes):
                for whole in (False, True):

                    @pl.when((plane == q) & (to_ahead == whole))
                    def _():
                        act(x_copy(f, n, q, whole))

        def x_send(f, n):
            x_each(f, n, ~ahead, lambda copy: copy.start())

        def core_copy(f, n):
            first = pl.multiple_of(plane * block + sibling * rows, rows)
            return pltpu.make_async_remote_copy(
                src_ref=column.at[f * here + n, pl.ds(first, window), :],
                dst_ref=twin.at[0, f * here + n],
                send_sem=send_c.at[0, f, n],
                recv_sem=recv_c.at[0, f, n],
                device_id={"frames": plane * PLANE + sibling},
            )

        def pass_copy(f, n):
            first = pl.multiple_of((1 - core) * rows, rows)
            return pltpu.make_async_remote_copy(
                src_ref=beside.at[f * here + n, pl.ds(first, window), :],
                dst_ref=twin.at[1, f * here + n],
                send_sem=send_c.at[1, f, n],
                recv_sem=recv_c.at[1, f, n],
                device_id={"frames": plane * PLANE + sibling},
            )

        load_down_t.wait()
        for n in range(here):
            for part in range(chunks):
                piece(n, part).wait()
                where = slice(part * (IMG // chunks), (part + 1) * (IMG // chunks))
                half[n, where] = jnp.dot(
                    video[n, where], down_t[...], preferred_element_type=jnp.float32
                ).astype(jnp.bfloat16)
            if n == 0:
                load_down.wait()
            column[plane * here + n, REACH : REACH + QUART, :] = jnp.dot(
                down[...], half[n], preferred_element_type=jnp.float32
            ).astype(jnp.bfloat16)
            if n == 0:
                pl.semaphore_wait(barrier, planes + 1)
            x_send(plane, n)
            core_copy(plane, n).start()
            for i in ORDERS[min(n, 1)]:
                if i < planes - 1:
                    z_send(n, others[i])

        counts = [jnp.int32(0)] * NSEG
        for t in range(frames):
            for s in range(NSEG):
                counts[s] = counts[s] + jnp.where(segments[t] == s, 1, 0)
        picked, first = [], jnp.int32(0)
        for s in range(NSEG):
            rest = picks[s]
            for bit in reversed(range((PICK_LIMIT - 1).bit_length())):
                rest = jnp.where(rest >= counts[s] * (1 << bit), rest - counts[s] * (1 << bit), rest)
            picked.append(first + rest)
            first = first + counts[s]

        lag = lax.broadcasted_iota(jnp.int32, (frames, frames), 0) - lax.broadcasted_iota(
            jnp.int32, (frames, frames), 1
        )
        toeplitz = jnp.zeros((frames, frames), jnp.float32)
        tap_row = taps[...].astype(jnp.float32)
        for k in range(min(taps.shape[1], frames)):
            toeplitz = jnp.where(lag == k, tap_row[:, k : k + 1], toeplitz)
        owner = lax.broadcasted_iota(jnp.int32, (total, frames), 0) // rows
        repeat = jnp.where(
            owner == lax.broadcasted_iota(jnp.int32, (total, frames), 1), 1.0, 0.0
        ).astype(jnp.bfloat16)
        tall = jnp.dot(
            repeat, toeplitz.astype(jnp.bfloat16), preferred_element_type=jnp.float32
        ).astype(jnp.bfloat16)
        wide = lax.dot_general(
            tall, repeat, (((1,), (1,)), ((), ())), preferred_element_type=jnp.float32
        )
        same = (
            lax.broadcasted_iota(jnp.int32, (total, total), 0) % rows
            == lax.broadcasted_iota(jnp.int32, (total, total), 1) % rows
        )
        matrix[...] = jnp.where(same, wide, 0.0).astype(jnp.bfloat16)

        def stack_one(place, block):
            stacked[place] = (
                jnp.dot(left[...], block, preferred_element_type=jnp.float32)
                .astype(jnp.bfloat16)
                .reshape(ORIENT * 2, rows, QUART)
            )

        def coefficients(where):
            tall_rows = planes * here * rows
            total_power = [0.0] * strips
            for o in range(ORIENT):
                even = stacked[:, where, :, 2 * o].reshape(tall_rows, QUART)
                odd = stacked[:, where, :, 2 * o + 1].reshape(tall_rows, QUART)

                def times(left_part, which):
                    return jnp.dot(left_part, right[o, which], preferred_element_type=jnp.float32)

                real = (times(even, 0) - times(odd, 1)).astype(jnp.bfloat16)
                imag = (times(even, 1) + times(odd, 0)).astype(jnp.bfloat16)
                wide_real, wide_imag = real.astype(jnp.float32), imag.astype(jnp.float32)
                power = wide_real * wide_real + wide_imag * wide_imag
                slot = slice(o % 2 * STRIP, (o % 2 + 1) * STRIP)
                imag_slot = slice(QUART + o % 2 * STRIP, QUART + (o % 2 + 1) * STRIP)
                for h in range(strips):
                    columns = slice(h * STRIP, (h + 1) * STRIP)
                    total_power[h] = total_power[h] + power[:, columns]

                    def split(value):
                        return value[:, columns].reshape(planes, here, rows, STRIP)

                    for p in range(planes):
                        at = pl.ds((p * PLANE + where) * here, here)
                        coeffs[h, at, o // 2, :, slot] = split(real)[p]
                        coeffs[h, at, o // 2, :, imag_slot] = split(imag)[p]
                        powers[h, at, o // 2, :, slot] = split(power)[p]
            for h in range(strips):
                whole = (total_power[h] + 1.0).reshape(planes, here, rows, STRIP)
                for p in range(planes):
                    denom[h, pl.ds((p * PLANE + where) * here, here)] = whole[p]

        own_rows = pl.ds(pl.multiple_of(plane * block + spot * rows, rows), window)
        core_rows = pl.ds(pl.multiple_of(core * rows, rows), window)

        def stack_column(f, n):
            stack_one((f, spot, n), column[f * here + n, own_rows, :])

        def stack_twin(f, n):
            stack_one((f, sibling, n), twin[0, f * here + n])

        def stack_sibling(f, n):
            core_copy(f, n).wait_recv()
            stack_twin(f, n)

        def x_wait(f, n):
            x_each(f, n, ahead, lambda copy: copy.wait_recv())

        def stack_beside(f, n):
            stack_one((f, across, n), beside[f * here + n, core_rows, :])

        def stack_passed(f, n):
            stack_one((f, flip(across, 1), n), twin[1, f * here + n])

        def stack_across(f, n):
            pass_copy(f, n).start()
            stack_beside(f, n)

        def stack_last(f, n):
            pass_copy(f, n).wait_recv()
            stack_passed(f, n)

        events = [(plane, n) for n in range(here)] + [
            (others[i], n)
            for n in range(here)
            for i in ORDERS[min(n, 1)]
            if i < planes - 1
        ]
        held_back = len(events) - LAG
        for i, (f, n) in enumerate(events):
            if i >= here:
                z_part(f, n, plane, lambda copy: copy.wait_recv())
                x_send(f, n)

                @pl.when(ahead)
                def _():
                    core_copy(f, n).start()

            if i == min(LAG, DUE):
                x_wait(*events[0])
            if i == DUE:
                for m in range(here):
                    late_own(m, lambda copy: copy.start())

            @pl.when(ahead)
            def _():
                stack_column(f, n)
                if i >= 1:
                    stack_sibling(*events[i - 1])
                if i >= LAG:
                    if i > LAG:
                        x_wait(*events[i - LAG])
                    stack_across(*events[i - LAG])
                if i >= LAG + 1:
                    stack_last(*events[i - LAG - 1])

        @pl.when(~ahead)
        def _():
            for f, n in events[here:]:
                late_wait(f, n, True)
                core_copy(f, n).start()
            for event in events:
                stack_column(*event)
            for f, n in events[:-1]:
                core_copy(f, n).wait_recv()
            for event in events[:-1]:
                stack_twin(*event)
            for i, (f, n) in enumerate(events[:held_back]):
                if i:
                    x_wait(f, n)
                late_wait(f, n, False)
                pass_copy(f, n).start()
            for event in events[:held_back]:
                stack_beside(*event)
            for f, n in events[: held_back - 1]:
                pass_copy(f, n).wait_recv()
            for event in events[: held_back - 1]:
                stack_passed(*event)

        stack_sibling(*events[-1])
        load_right.wait()
        coefficients(spot)
        coefficients(sibling)
        for f, n in events[held_back:]:
            x_wait(f, n)

            @pl.when(~ahead)
            def _():
                late_wait(f, n, False)

            pass_copy(f, n).start()
        for event in events[held_back:]:
            stack_beside(*event)
        coefficients(across)
        for f, n in events[held_back - 1 :]:
            pass_copy(f, n).wait_recv()
        for event in events[held_back - 1 :]:
            stack_passed(*event)
        coefficients(flip(across, 1))

        here_rows = pl.ds(pl.multiple_of(me * rows, rows), rows)

        def phases(h):
            @pl.loop(0, frames // UNROLL)
            def _(step):
                for u in range(UNROLL):
                    t = step * UNROLL + u
                    ref = picked[NSEG - 1]
                    for s in range(NSEG - 1):
                        ref = jnp.where(segments[t] == s, picked[s], ref)
                    ones = coeffs[h, t].astype(jnp.float32)
                    base = coeffs[h, ref].astype(jnp.float32)
                    prod_imag = ones[..., QUART:] * base[..., :QUART] - ones[..., :QUART] * base[..., QUART:]
                    signal = prod_imag * lax.rsqrt(powers[h, t] * powers[h, ref] + 1.0)
                    phase[:, t] = signal.astype(jnp.bfloat16)

        def return_copy(h, j):
            to = peer(j)
            return pltpu.make_async_remote_copy(
                src_ref=moved.at[h, pl.ds(to * here, here)],
                dst_ref=out_hbm.at[:, here_rows, h * STRIP : (h + 1) * STRIP],
                send_sem=send_b.at[h, j],
                recv_sem=recv_b.at[h, j],
                device_id={"frames": to},
            )

        def store(h):
            return pltpu.make_async_copy(
                moved.at[h, pl.ds(me * here, here)],
                out_hbm.at[:, here_rows, h * STRIP : (h + 1) * STRIP],
                store_sem.at[h],
            )

        crowd = parts // 2
        near = me // crowd

        def filter_half(h, number):
            span = slice(number * (frames // 2), (number + 1) * (frames // 2))
            until = (number + 1) * (total // 2)
            numer = 0.0
            for q in range(ORIENT // 2):
                filtered = (
                    jnp.dot(
                        matrix[number * (total // 2) : until, :until],
                        phase[q].reshape(total, QUART)[:until],
                        preferred_element_type=jnp.float32,
                    )
                    .astype(jnp.bfloat16)
                    .astype(jnp.float32)
                    .reshape(frames // 2, rows, QUART)
                )
                numer = numer + powers[h, span, q] * filtered
            numer = numer[..., :STRIP] + numer[..., STRIP:]
            moved[h, span] = (numer / denom[h, span]).astype(jnp.bfloat16)

        for h in range(strips):
            phases(h)
            for close in (False, True):
                for number in range(2):

                    @pl.when((near == number) == close)
                    def _():
                        filter_half(h, number)

                base_to = (near if close else 1 - near) * crowd

                @pl.loop(1 if close else 0, crowd)
                def _(k):
                    to = base_to + lax.rem(me + k, crowd)
                    return_copy(h, lax.rem(to + parts - me, parts)).start()

            store(h).start()

        for f, n in events:
            x_each(f, n, ~ahead, lambda copy: copy.wait_send())
            core_copy(f, n).wait_send()
            pass_copy(f, n).wait_send()
        for n in range(here):
            for to in others:
                z_part(plane, n, to, lambda copy: copy.wait_send())
            late_own(n, lambda copy: copy.wait_send())

        for h in range(strips):

            @pl.loop(1, parts)
            def _(j):
                return_copy(h, j).wait_recv()
                return_copy(h, j).wait_send()

            store(h).wait()

    bf16, f32, dma = jnp.bfloat16, jnp.float32, pltpu.SemaphoreType.DMA
    anywhere = pl.BlockSpec(memory_space=pl.ANY)
    vmem = pl.BlockSpec(memory_space=pltpu.VMEM)
    smem = pl.BlockSpec(memory_space=pltpu.SMEM)
    return pl.pallas_call(
        kernel,
        out_shape=jax.ShapeDtypeStruct((here, QUART, QUART), bf16),
        in_specs=[smem, smem, vmem, anywhere, anywhere, anywhere, vmem, anywhere],
        out_specs=anywhere,
        scratch_shapes=[
            pltpu.VMEM((here, IMG, IMG), bf16),
            pltpu.VMEM((QUART, IMG), bf16),
            pltpu.VMEM((IMG, QUART), bf16),
            pltpu.VMEM((ORIENT, 2, QUART, QUART), bf16),
            pltpu.VMEM((here, IMG, QUART), bf16),
            pltpu.VMEM((planes * here, QUART + 2 * REACH, QUART), bf16),
            pltpu.VMEM((planes * here, pair_window, QUART), bf16),
            pltpu.VMEM((2, planes * here, window, QUART), bf16),
            pltpu.VMEM((planes, PLANE, here, ORIENT * 2, rows, QUART), bf16),
            pltpu.VMEM((strips, frames, ORIENT // 2, rows, 2 * QUART), bf16),
            pltpu.VMEM((strips, frames, ORIENT // 2, rows, QUART), f32),
            pltpu.VMEM((ORIENT // 2, frames, rows, QUART), bf16),
            pltpu.VMEM((total, total), bf16),
            pltpu.VMEM((strips, frames, rows, STRIP), f32),
            pltpu.VMEM((strips, frames, rows, STRIP), bf16),
            dma((3 + here * chunks,)),
            dma((strips,)),
            dma((planes, here)),
            dma((planes, here)),
            dma((planes, here)),
            dma((2, planes, here)),
            dma((planes, here)),
            dma((planes, here)),
            dma((2, planes, here)),
            dma((2, planes, here)),
            dma((strips, parts)),
            dma((strips, parts)),
        ],
        compiler_params=pltpu.CompilerParams(
            collective_id=0, has_side_effects=True, vmem_limit_bytes=60 * 1024 * 1024
        ),
    )


def kernel_body(parts, video_frames, segments, ref_pick, band_taps):
    here = video_frames.shape[0]
    rows = QUART // parts
    down = down_table()
    return make_kernel(parts, here, rows)(
        segments,
        ref_pick,
        band_taps[None, :],
        video_frames,
        jnp.asarray(down),
        jnp.asarray(np.ascontiguousarray(down.T)),
        jnp.asarray(left_window(rows)),
        jnp.asarray(right_tables()),
    ).astype(jnp.float32)


def solution(mesh):
    parts = mesh.shape["frames"]
    if QUART % parts == 0 and (QUART // parts) % 16 == 0 and parts in (4, 8, 16):
        chosen = lambda *args: kernel_body(parts, *args)
    else:
        chosen = body
    in_specs = (P(("groups", "frames"), None, None), P("groups"), P("groups"), P())
    out_specs = P(("groups", "frames"), None, None)
    return jax.shard_map(chosen, mesh=mesh, in_specs=in_specs, out_specs=out_specs, check_vma=False)
```

```python
import math

import jax
import numpy as np
import jax.numpy as jnp
from jax import lax
from jax.experimental import pallas as pl
from jax.experimental.pallas import tpu as pltpu
from jax.sharding import PartitionSpec as P

IMG = 1024
ORIENT = 4
NSEG = 4
QUART = 256


blur_sigma = 2.0
gabor_sigma = 2.0
wave_number = math.pi / 2.0
gabor_gain = 2.0


def spread(x, axis, root):
    mine = lax.axis_index(axis) == root
    return lax.psum(jnp.where(mine, x, jnp.zeros_like(x)), axis)


def make_down(full_size, quarter):
    position = jnp.arange(quarter, dtype=jnp.float32)[:, None]
    columns = jnp.arange(full_size, dtype=jnp.float32)[None, :]
    offset_grid = columns - 4.0 * position - 1.5
    weight = jnp.exp(-offset_grid * offset_grid / (2.0 * blur_sigma * blur_sigma))
    return (weight / jnp.sum(weight, axis=1, keepdims=True)).astype(jnp.bfloat16)


def gabor_tables(quarter, orient):
    position = jnp.arange(quarter, dtype=jnp.float32)
    offset_grid = position[None, :] - position[:, None]
    envelope = gabor_gain * jnp.exp(-offset_grid * offset_grid / (2.0 * gabor_sigma * gabor_sigma))
    angles = jnp.arange(orient, dtype=jnp.float32) * (math.pi / orient)
    wave_x = wave_number * jnp.cos(angles)
    wave_y = wave_number * jnp.sin(angles)
    phase_y = wave_y[:, None, None] * offset_grid[None]
    left_table = jnp.stack([envelope * jnp.cos(phase_y), envelope * jnp.sin(phase_y)], axis=2)
    left_table = left_table.reshape(orient * quarter * 2, quarter).astype(jnp.bfloat16)
    phase_x = wave_x[:, None, None] * (-offset_grid)[None]
    real_part = envelope * jnp.cos(phase_x)
    imag_part = envelope * jnp.sin(phase_x)
    upper_half = jnp.concatenate([real_part, imag_part], axis=2)
    lower_half = jnp.concatenate([-imag_part, real_part], axis=2)
    right_table = jnp.concatenate([upper_half, lower_half], axis=1).astype(jnp.bfloat16)
    return (left_table, right_table)


def phase_terms(coeffs, per_frame):
    quarter = coeffs.shape[-1] // 2
    coeff_real = coeffs[..., :quarter].astype(jnp.float32)
    coeff_imag = coeffs[..., quarter:].astype(jnp.float32)
    ref_real = per_frame[..., :quarter].astype(jnp.float32)
    ref_imag = per_frame[..., quarter:].astype(jnp.float32)
    prod_real = coeff_real * ref_real + coeff_imag * ref_imag
    prod_imag = coeff_imag * ref_real - coeff_real * ref_imag
    phase_signal = (
        prod_imag / jnp.sqrt(prod_real * prod_real + prod_imag * prod_imag + 1.0)
    ).astype(jnp.bfloat16)
    amplitude = coeff_real * coeff_real + coeff_imag * coeff_imag
    return (phase_signal, amplitude)


def taps_matrix(band_taps, frame_count):
    frame_index = jnp.arange(frame_count, dtype=jnp.int32)
    lag_grid = frame_index[:, None] - frame_index[None, :]
    one_hot = (
        lag_grid[:, :, None] == jnp.arange(band_taps.shape[0], dtype=jnp.int32)[None, None, :]
    ).astype(jnp.float32)
    return jnp.einsum("tsk,k->ts", one_hot, band_taps.astype(jnp.float32)).astype(jnp.bfloat16)


def segment_refs(segments, ref_pick, segment_count):
    numbers = jnp.arange(segment_count, dtype=jnp.int32)
    starts = jnp.sum((segments[None, :] < numbers[:, None]).astype(jnp.int32), axis=1)
    counts = jnp.sum((segments[None, :] == numbers[:, None]).astype(jnp.int32), axis=1)
    return starts + ref_pick % counts


def body(video_frames, segments, ref_pick, band_taps):
    frames_here = video_frames.shape[0]
    down_matrix = make_down(IMG, QUART)
    left_table, right_table = gabor_tables(QUART, ORIENT)

    def reduce_frames(pictures):
        half_done = jnp.einsum(
            "nia,qa->niq", pictures, down_matrix, preferred_element_type=jnp.float32
        ).astype(jnp.bfloat16)
        return jnp.einsum(
            "qi,nik->nqk", down_matrix, half_done, preferred_element_type=jnp.float32
        ).astype(jnp.bfloat16)

    def filter_frames(reduced):
        stacked = jnp.einsum(
            "ra,nak->nrk", left_table, reduced, preferred_element_type=jnp.float32
        ).astype(jnp.bfloat16)
        stacked = stacked.reshape(reduced.shape[0], ORIENT, QUART, 2 * QUART)
        return jnp.einsum(
            "noya,oab->noyb", stacked, right_table, preferred_element_type=jnp.float32
        ).astype(jnp.bfloat16)

    small_own = reduce_frames(video_frames)
    coeff_own = filter_frames(small_own)
    ref_frames = segment_refs(segments, ref_pick, NSEG)
    gathered = []
    for segment in range(NSEG):
        root_index = ref_frames[segment] // frames_here
        local_index = ref_frames[segment] % frames_here
        payload = lax.dynamic_index_in_dim(video_frames, local_index, 0, keepdims=False)
        gathered.append(spread(payload, "frames", root_index))
    ref_coeff = filter_frames(reduce_frames(jnp.stack(gathered)))
    first_frame = lax.axis_index("frames") * frames_here
    own_ids = lax.dynamic_slice_in_dim(segments, first_frame, frames_here)
    select = (own_ids[:, None] == jnp.arange(NSEG, dtype=jnp.int32)[None, :]).astype(jnp.bfloat16)
    per_frame = jnp.dot(select, ref_coeff.reshape(NSEG, -1), preferred_element_type=jnp.float32)
    per_frame = per_frame.astype(jnp.bfloat16).reshape(coeff_own.shape)
    phase_signal, amplitude = phase_terms(coeff_own, per_frame)
    phase_signal = phase_signal.reshape(frames_here, ORIENT, QUART * QUART)
    pixel_rows = lax.all_to_all(phase_signal, "frames", split_axis=2, concat_axis=0, tiled=True)
    matrix = taps_matrix(band_taps, pixel_rows.shape[0])
    filtered = jnp.einsum(
        "ts,sop->top", matrix, pixel_rows, preferred_element_type=jnp.float32
    ).astype(jnp.bfloat16)
    filtered = lax.all_to_all(filtered, "frames", split_axis=0, concat_axis=2, tiled=True)
    filtered = filtered.reshape(frames_here, ORIENT, QUART, QUART).astype(jnp.float32)
    return jnp.sum(amplitude * filtered, axis=1) / (jnp.sum(amplitude, axis=1) + 1.0)


PICK_LIMIT = 4096
REACH = 32


def down_table():
    position = np.arange(QUART, dtype=np.float32)[:, None]
    columns = np.arange(IMG, dtype=np.float32)[None, :]
    offset = columns - np.float32(4.0) * position - np.float32(1.5)
    weight = np.exp(-offset * offset / np.float32(2.0 * blur_sigma * blur_sigma))
    return (weight / np.sum(weight, axis=1, keepdims=True)).astype(jnp.bfloat16)


def waves():
    angles = np.arange(ORIENT, dtype=np.float32) * np.float32(math.pi / ORIENT)
    return np.float32(wave_number) * np.cos(angles), np.float32(wave_number) * np.sin(angles)


def gabor_envelope(offset):
    return np.float32(gabor_gain) * np.exp(-offset * offset / np.float32(2.0 * gabor_sigma * gabor_sigma))


def left_window(rows):
    offset = (
        np.arange(rows + 2 * REACH, dtype=np.float32)[None, :]
        - REACH
        - np.arange(rows, dtype=np.float32)[:, None]
    )
    envelope = gabor_envelope(offset)
    phase = waves()[1][:, None, None] * offset[None]
    table = np.stack([envelope * np.cos(phase), envelope * np.sin(phase)], axis=1)
    return table.reshape(ORIENT * 2 * rows, -1).astype(jnp.bfloat16)


def right_tables():
    position = np.arange(QUART, dtype=np.float32)
    offset = position[:, None] - position[None, :]
    envelope = gabor_envelope(offset)
    phase = waves()[0][:, None, None] * offset[None]
    real, imag = envelope * np.cos(phase), envelope * np.sin(phase)
    return np.stack([real, imag], axis=1).astype(jnp.bfloat16)


PLANE = 4
PAIR = 2
LAG = 3
DUE = 3
STRIP = 128
UNROLL = 4
ORDERS = ((0, 1, 2), (0, 1, 2))


def flip(number, bits):
    step = 1
    while step <= bits:
        if bits & step:
            number = number + step - 2 * step * ((number // step) % 2)
        step *= 2
    return number


def make_kernel(parts, here, rows):
    frames = parts * here
    planes = parts // PLANE
    window = rows + 2 * REACH
    pair_window = PAIR * rows + 2 * REACH
    total = frames * rows
    chunks = 2
    strips = QUART // STRIP

    def kernel(
        segments, picks, taps, video_hbm, down_hbm, down_t_hbm, left, right_hbm, out_hbm,
        video, down, down_t, right, half, column, beside, twin, stacked, coeffs,
        powers, phase, matrix, denom, moved,
        load_sem, store_sem, send_z, recv_z, send_l, recv_l, send_x, recv_x, send_c, recv_c, send_b, recv_b,
    ):
        me = lax.axis_index("frames")
        plane, spot = me // PLANE, me % PLANE
        across, sibling = flip(spot, PAIR), flip(spot, 1)
        side, core = spot // PAIR, spot % PAIR
        barrier = pltpu.get_barrier_semaphore()

        def peer(j):
            return lax.rem(me + j, parts)

        def piece(n, part):
            height = IMG // chunks
            where = pl.ds(part * height, height)
            return pltpu.make_async_copy(
                video_hbm.at[n, where], video.at[n, where], load_sem.at[3 + n * chunks + part]
            )

        load_down = pltpu.make_async_copy(down_hbm, down, load_sem.at[1])
        load_down_t = pltpu.make_async_copy(down_t_hbm, down_t, load_sem.at[0])
        load_right = pltpu.make_async_copy(right_hbm, right, load_sem.at[2])
        load_down_t.start()
        for n in range(here):
            for part in range(chunks):
                piece(n, part).start()
            if n == 0:
                load_down.start()
        load_right.start()

        def greet(where):
            pl.semaphore_signal(barrier, inc=1, device_id={"frames": where})

        others = [flip(plane, j) for j in range(1, planes)]
        for to in reversed(others):
            greet(to * PLANE + spot)
        greet(plane * PLANE + across)
        greet(plane * PLANE + sibling)

        blank = jnp.zeros((planes * here, REACH, QUART), jnp.bfloat16)
        column[:, :REACH, :] = blank
        column[:, REACH + QUART :, :] = blank

        block = PLANE * rows
        low, high = REACH, REACH + QUART

        def early(q):
            return 0 if q < max(planes // 2, 1) else 1

        ahead = side == jnp.where(plane < max(planes // 2, 1), 0, 1)

        def bounds(first, last):
            return max(first, low), min(last, high)

        def early_rows(q):
            first = block * q + (PAIR * rows if early(q) else 0)
            return bounds(first, first + pair_window)

        def late_rows(q):
            first = block * q + (0 if early(q) else pair_window)
            return bounds(first, first + PAIR * rows)

        def z_copy(f, n, q):
            first, last = early_rows(q)
            part = column.at[f * here + n, first:last, :]
            return pltpu.make_async_remote_copy(
                src_ref=part,
                dst_ref=part,
                send_sem=send_z.at[q, n],
                recv_sem=recv_z.at[f, n],
                device_id={"frames": q * PLANE + spot},
            )

        def z_part(f, n, to, act):
            for q in range(planes):

                @pl.when(to == q)
                def _():
                    act(z_copy(f, n, q))

        def z_send(n, to):
            z_part(plane, n, to, lambda copy: copy.start())

        def late_copy(f, n, q, straight):
            first, last = late_rows(q)
            inside = 0 if early(q) else pair_window - PAIR * rows
            inside = inside + first - (block * q + (0 if early(q) else pair_window))
            target = (
                column.at[f * here + n, first:last, :]
                if straight
                else beside.at[f * here + n, inside : inside + last - first, :]
            )
            other_side = 1 - early(q)
            return pltpu.make_async_remote_copy(
                src_ref=column.at[f * here + n, first:last, :],
                dst_ref=target,
                send_sem=send_l.at[q, n],
                recv_sem=recv_l.at[0 if straight else 1, f, n],
                device_id={"frames": q * PLANE + other_side * PAIR + core},
            )

        def has_late(q):
            first, last = late_rows(q)
            return last > first

        def late_own(n, act):
            for q in range(planes):
                if has_late(q):

                    @pl.when((side == 1 - early(q)) & (plane != q))
                    def _():
                        act(late_copy(plane, n, q, True))

                    @pl.when(side == early(q))
                    def _():
                        act(late_copy(plane, n, q, False))

        def late_wait(f, n, straight):
            for q in range(planes):
                if has_late(q):

                    @pl.when(plane == q)
                    def _():
                        late_copy(f, n, q, straight).wait_recv()

        def x_copy(f, n, q, whole):
            first = block * q + (PAIR * rows if early(q) else 0)
            inside, size = 0, pair_window
            if not whole:
                first, size = block * q + PAIR * rows, pair_window - PAIR * rows
                inside = PAIR * rows if early(q) else 0
            return pltpu.make_async_remote_copy(
                src_ref=column.at[f * here + n, first : first + size, :],
                dst_ref=beside.at[f * here + n, inside : inside + size, :],
                send_sem=send_x.at[f, n],
                recv_sem=recv_x.at[f, n],
                device_id={"frames": plane * PLANE + across},
            )

        def x_each(f, n, to_ahead, act):
            for q in range(planes):
                for whole in (False, True):

                    @pl.when((plane == q) & (to_ahead == whole))
                    def _():
                        act(x_copy(f, n, q, whole))

        def x_send(f, n):
            x_each(f, n, ~ahead, lambda copy: copy.start())

        def core_copy(f, n):
            first = pl.multiple_of(plane * block + sibling * rows, rows)
            return pltpu.make_async_remote_copy(
                src_ref=column.at[f * here + n, pl.ds(first, window), :],
                dst_ref=twin.at[0, f * here + n],
                send_sem=send_c.at[0, f, n],
                recv_sem=recv_c.at[0, f, n],
                device_id={"frames": plane * PLANE + sibling},
            )

        def pass_copy(f, n):
            first = pl.multiple_of((1 - core) * rows, rows)
            return pltpu.make_async_remote_copy(
                src_ref=beside.at[f * here + n, pl.ds(first, window), :],
                dst_ref=twin.at[1, f * here + n],
                send_sem=send_c.at[1, f, n],
                recv_sem=recv_c.at[1, f, n],
                device_id={"frames": plane * PLANE + sibling},
            )

        load_down_t.wait()
        for n in range(here):
            for part in range(chunks):
                piece(n, part).wait()
                where = slice(part * (IMG // chunks), (part + 1) * (IMG // chunks))
                half[n, where] = jnp.dot(
                    video[n, where], down_t[...], preferred_element_type=jnp.float32
                ).astype(jnp.bfloat16)
            if n == 0:
                load_down.wait()
            column[plane * here + n, REACH : REACH + QUART, :] = jnp.dot(
                down[...], half[n], preferred_element_type=jnp.float32
            ).astype(jnp.bfloat16)
            if n == 0:
                pl.semaphore_wait(barrier, planes + 1)
            x_send(plane, n)
            core_copy(plane, n).start()
            for i in ORDERS[min(n, 1)]:
                if i < planes - 1:
                    z_send(n, others[i])

        counts = [jnp.int32(0)] * NSEG
        for t in range(frames):
            for s in range(NSEG):
                counts[s] = counts[s] + jnp.where(segments[t] == s, 1, 0)
        picked, first = [], jnp.int32(0)
        for s in range(NSEG):
            rest = picks[s]
            for bit in reversed(range((PICK_LIMIT - 1).bit_length())):
                rest = jnp.where(rest >= counts[s] * (1 << bit), rest - counts[s] * (1 << bit), rest)
            picked.append(first + rest)
            first = first + counts[s]

        lag = lax.broadcasted_iota(jnp.int32, (frames, frames), 0) - lax.broadcasted_iota(
            jnp.int32, (frames, frames), 1
        )
        toeplitz = jnp.zeros((frames, frames), jnp.float32)
        tap_row = taps[...].astype(jnp.float32)
        for k in range(min(taps.shape[1], frames)):
            toeplitz = jnp.where(lag == k, tap_row[:, k : k + 1], toeplitz)
        owner = lax.broadcasted_iota(jnp.int32, (total, frames), 0) // rows
        repeat = jnp.where(
            owner == lax.broadcasted_iota(jnp.int32, (total, frames), 1), 1.0, 0.0
        ).astype(jnp.bfloat16)
        tall = jnp.dot(
            repeat, toeplitz.astype(jnp.bfloat16), preferred_element_type=jnp.float32
        ).astype(jnp.bfloat16)
        wide = lax.dot_general(
            tall, repeat, (((1,), (1,)), ((), ())), preferred_element_type=jnp.float32
        )
        same = (
            lax.broadcasted_iota(jnp.int32, (total, total), 0) % rows
            == lax.broadcasted_iota(jnp.int32, (total, total), 1) % rows
        )
        matrix[...] = jnp.where(same, wide, 0.0).astype(jnp.bfloat16)

        def stack_one(place, block):
            stacked[place] = (
                jnp.dot(left[...], block, preferred_element_type=jnp.float32)
                .astype(jnp.bfloat16)
                .reshape(ORIENT * 2, rows, QUART)
            )

        def coefficients(where):
            tall_rows = planes * here * rows
            total_power = [0.0] * strips
            for o in range(ORIENT):
                even = stacked[:, where, :, 2 * o].reshape(tall_rows, QUART)
                odd = stacked[:, where, :, 2 * o + 1].reshape(tall_rows, QUART)

                def times(left_part, which):
                    return jnp.dot(left_part, right[o, which], preferred_element_type=jnp.float32)

                real = (times(even, 0) - times(odd, 1)).astype(jnp.bfloat16)
                imag = (times(even, 1) + times(odd, 0)).astype(jnp.bfloat16)
                wide_real, wide_imag = real.astype(jnp.float32), imag.astype(jnp.float32)
                power = wide_real * wide_real + wide_imag * wide_imag
                slot = slice(o % 2 * STRIP, (o % 2 + 1) * STRIP)
                imag_slot = slice(QUART + o % 2 * STRIP, QUART + (o % 2 + 1) * STRIP)
                for h in range(strips):
                    columns = slice(h * STRIP, (h + 1) * STRIP)
                    total_power[h] = total_power[h] + power[:, columns]

                    def split(value):
                        return value[:, columns].reshape(planes, here, rows, STRIP)

                    for p in range(planes):
                        at = pl.ds((p * PLANE + where) * here, here)
                        coeffs[h, at, o // 2, :, slot] = split(real)[p]
                        coeffs[h, at, o // 2, :, imag_slot] = split(imag)[p]
                        powers[h, at, o // 2, :, slot] = split(power)[p]
            for h in range(strips):
                whole = (total_power[h] + 1.0).reshape(planes, here, rows, STRIP)
                for p in range(planes):
                    denom[h, pl.ds((p * PLANE + where) * here, here)] = whole[p]

        own_rows = pl.ds(pl.multiple_of(plane * block + spot * rows, rows), window)
        core_rows = pl.ds(pl.multiple_of(core * rows, rows), window)

        def stack_column(f, n):
            stack_one((f, spot, n), column[f * here + n, own_rows, :])

        def stack_twin(f, n):
            stack_one((f, sibling, n), twin[0, f * here + n])

        def stack_sibling(f, n):
            core_copy(f, n).wait_recv()
            stack_twin(f, n)

        def x_wait(f, n):
            x_each(f, n, ahead, lambda copy: copy.wait_recv())

        def stack_beside(f, n):
            stack_one((f, across, n), beside[f * here + n, core_rows, :])

        def stack_passed(f, n):
            stack_one((f, flip(across, 1), n), twin[1, f * here + n])

        def stack_across(f, n):
            pass_copy(f, n).start()
            stack_beside(f, n)

        def stack_last(f, n):
            pass_copy(f, n).wait_recv()
            stack_passed(f, n)

        events = [(plane, n) for n in range(here)] + [
            (others[i], n)
            for n in range(here)
            for i in ORDERS[min(n, 1)]
            if i < planes - 1
        ]
        held_back = len(events) - LAG
        for i, (f, n) in enumerate(events):
            if i >= here:
                z_part(f, n, plane, lambda copy: copy.wait_recv())
                x_send(f, n)

                @pl.when(ahead)
                def _():
                    core_copy(f, n).start()

            if i == min(LAG, DUE):
                x_wait(*events[0])
            if i == DUE:
                for m in range(here):
                    late_own(m, lambda copy: copy.start())

            @pl.when(ahead)
            def _():
                stack_column(f, n)
                if i >= 1:
                    stack_sibling(*events[i - 1])
                if i >= LAG:
                    if i > LAG:
                        x_wait(*events[i - LAG])
                    stack_across(*events[i - LAG])
                if i >= LAG + 1:
                    stack_last(*events[i - LAG - 1])

        @pl.when(~ahead)
        def _():
            middle = here + planes - 1
            for group in (range(middle), range(middle, len(events))):
                forward = [i for i in group if i < held_back]
                for i in group:
                    if i >= here:
                        late_wait(*events[i], True)
                        core_copy(*events[i]).start()
                for i in forward:
                    if i:
                        x_wait(*events[i])
                    late_wait(*events[i], False)
                    pass_copy(*events[i]).start()
                for i in group:
                    stack_column(*events[i])
                for i in forward:
                    stack_beside(*events[i])
                twins = [i for i in group if i < len(events) - 1]
                for i in twins:
                    core_copy(*events[i]).wait_recv()
                for i in twins:
                    stack_twin(*events[i])
                ready = [i for i in forward if i < held_back - 1]
                for i in ready:
                    pass_copy(*events[i]).wait_recv()
                for i in ready:
                    stack_passed(*events[i])

        stack_sibling(*events[-1])
        load_right.wait()
        coefficients(spot)
        coefficients(sibling)
        for f, n in events[held_back:]:
            x_wait(f, n)

            @pl.when(~ahead)
            def _():
                late_wait(f, n, False)

            pass_copy(f, n).start()
        for event in events[held_back:]:
            stack_beside(*event)
        coefficients(across)
        for f, n in events[held_back - 1 :]:
            pass_copy(f, n).wait_recv()
        for event in events[held_back - 1 :]:
            stack_passed(*event)
        coefficients(flip(across, 1))

        here_rows = pl.ds(pl.multiple_of(me * rows, rows), rows)

        def phases(h):
            @pl.loop(0, frames // UNROLL)
            def _(step):
                for u in range(UNROLL):
                    t = step * UNROLL + u
                    ref = picked[NSEG - 1]
                    for s in range(NSEG - 1):
                        ref = jnp.where(segments[t] == s, picked[s], ref)
                    ones = coeffs[h, t].astype(jnp.float32)
                    base = coeffs[h, ref].astype(jnp.float32)
                    prod_imag = ones[..., QUART:] * base[..., :QUART] - ones[..., :QUART] * base[..., QUART:]
                    signal = prod_imag * lax.rsqrt(powers[h, t] * powers[h, ref] + 1.0)
                    phase[:, t] = signal.astype(jnp.bfloat16)

        def return_copy(h, j):
            to = peer(j)
            return pltpu.make_async_remote_copy(
                src_ref=moved.at[h, pl.ds(to * here, here)],
                dst_ref=out_hbm.at[:, here_rows, h * STRIP : (h + 1) * STRIP],
                send_sem=send_b.at[h, j],
                recv_sem=recv_b.at[h, j],
                device_id={"frames": to},
            )

        def store(h):
            return pltpu.make_async_copy(
                moved.at[h, pl.ds(me * here, here)],
                out_hbm.at[:, here_rows, h * STRIP : (h + 1) * STRIP],
                store_sem.at[h],
            )

        crowd = parts // 2
        near = me // crowd

        def filter_half(h, number):
            span = slice(number * (frames // 2), (number + 1) * (frames // 2))
            until = (number + 1) * (total // 2)
            numer = 0.0
            for q in range(ORIENT // 2):
                filtered = (
                    jnp.dot(
                        matrix[number * (total // 2) : until, :until],
                        phase[q].reshape(total, QUART)[:until],
                        preferred_element_type=jnp.float32,
                    )
                    .astype(jnp.bfloat16)
                    .astype(jnp.float32)
                    .reshape(frames // 2, rows, QUART)
                )
                numer = numer + powers[h, span, q] * filtered
            numer = numer[..., :STRIP] + numer[..., STRIP:]
            moved[h, span] = (numer / denom[h, span]).astype(jnp.bfloat16)

        for h in range(strips):
            phases(h)
            for close in (False, True):
                for number in range(2):

                    @pl.when((near == number) == close)
                    def _():
                        filter_half(h, number)

                base_to = (near if close else 1 - near) * crowd

                @pl.loop(1 if close else 0, crowd)
                def _(k):
                    to = base_to + lax.rem(me + k, crowd)
                    return_copy(h, lax.rem(to + parts - me, parts)).start()

            store(h).start()

        for f, n in events:
            x_each(f, n, ~ahead, lambda copy: copy.wait_send())
            core_copy(f, n).wait_send()
            pass_copy(f, n).wait_send()
        for n in range(here):
            for to in others:
                z_part(plane, n, to, lambda copy: copy.wait_send())
            late_own(n, lambda copy: copy.wait_send())

        for h in range(strips):

            @pl.loop(1, parts)
            def _(j):
                return_copy(h, j).wait_recv()
                return_copy(h, j).wait_send()

            store(h).wait()

    bf16, f32, dma = jnp.bfloat16, jnp.float32, pltpu.SemaphoreType.DMA
    anywhere = pl.BlockSpec(memory_space=pl.ANY)
    vmem = pl.BlockSpec(memory_space=pltpu.VMEM)
    smem = pl.BlockSpec(memory_space=pltpu.SMEM)
    return pl.pallas_call(
        kernel,
        out_shape=jax.ShapeDtypeStruct((here, QUART, QUART), bf16),
        in_specs=[smem, smem, vmem, anywhere, anywhere, anywhere, vmem, anywhere],
        out_specs=anywhere,
        scratch_shapes=[
            pltpu.VMEM((here, IMG, IMG), bf16),
            pltpu.VMEM((QUART, IMG), bf16),
            pltpu.VMEM((IMG, QUART), bf16),
            pltpu.VMEM((ORIENT, 2, QUART, QUART), bf16),
            pltpu.VMEM((here, IMG, QUART), bf16),
            pltpu.VMEM((planes * here, QUART + 2 * REACH, QUART), bf16),
            pltpu.VMEM((planes * here, pair_window, QUART), bf16),
            pltpu.VMEM((2, planes * here, window, QUART), bf16),
            pltpu.VMEM((planes, PLANE, here, ORIENT * 2, rows, QUART), bf16),
            pltpu.VMEM((strips, frames, ORIENT // 2, rows, 2 * QUART), bf16),
            pltpu.VMEM((strips, frames, ORIENT // 2, rows, QUART), f32),
            pltpu.VMEM((ORIENT // 2, frames, rows, QUART), bf16),
            pltpu.VMEM((total, total), bf16),
            pltpu.VMEM((strips, frames, rows, STRIP), f32),
            pltpu.VMEM((strips, frames, rows, STRIP), bf16),
            dma((3 + here * chunks,)),
            dma((strips,)),
            dma((planes, here)),
            dma((planes, here)),
            dma((planes, here)),
            dma((2, planes, here)),
            dma((planes, here)),
            dma((planes, here)),
            dma((2, planes, here)),
            dma((2, planes, here)),
            dma((strips, parts)),
            dma((strips, parts)),
        ],
        compiler_params=pltpu.CompilerParams(
            collective_id=0, has_side_effects=True, vmem_limit_bytes=60 * 1024 * 1024
        ),
    )


def kernel_body(parts, video_frames, segments, ref_pick, band_taps):
    here = video_frames.shape[0]
    rows = QUART // parts
    down = down_table()
    return make_kernel(parts, here, rows)(
        segments,
        ref_pick,
        band_taps[None, :],
        video_frames,
        jnp.asarray(down),
        jnp.asarray(np.ascontiguousarray(down.T)),
        jnp.asarray(left_window(rows)),
        jnp.asarray(right_tables()),
    ).astype(jnp.float32)


def solution(mesh):
    parts = mesh.shape["frames"]
    if QUART % parts == 0 and (QUART // parts) % 16 == 0 and parts in (4, 8, 16):
        chosen = lambda *args: kernel_body(parts, *args)
    else:
        chosen = body
    in_specs = (P(("groups", "frames"), None, None), P("groups"), P("groups"), P())
    out_specs = P(("groups", "frames"), None, None)
    return jax.shard_map(chosen, mesh=mesh, in_specs=in_specs, out_specs=out_specs, check_vma=False)
```

```python
import math

import jax
import numpy as np
import jax.numpy as jnp
from jax import lax
from jax.experimental import pallas as pl
from jax.experimental.pallas import tpu as pltpu
from jax.sharding import PartitionSpec as P

IMG = 1024
ORIENT = 4
NSEG = 4
QUART = 256


blur_sigma = 2.0
gabor_sigma = 2.0
wave_number = math.pi / 2.0
gabor_gain = 2.0


def spread(x, axis, root):
    mine = lax.axis_index(axis) == root
    return lax.psum(jnp.where(mine, x, jnp.zeros_like(x)), axis)


def make_down(full_size, quarter):
    position = jnp.arange(quarter, dtype=jnp.float32)[:, None]
    columns = jnp.arange(full_size, dtype=jnp.float32)[None, :]
    offset_grid = columns - 4.0 * position - 1.5
    weight = jnp.exp(-offset_grid * offset_grid / (2.0 * blur_sigma * blur_sigma))
    return (weight / jnp.sum(weight, axis=1, keepdims=True)).astype(jnp.bfloat16)


def gabor_tables(quarter, orient):
    position = jnp.arange(quarter, dtype=jnp.float32)
    offset_grid = position[None, :] - position[:, None]
    envelope = gabor_gain * jnp.exp(-offset_grid * offset_grid / (2.0 * gabor_sigma * gabor_sigma))
    angles = jnp.arange(orient, dtype=jnp.float32) * (math.pi / orient)
    wave_x = wave_number * jnp.cos(angles)
    wave_y = wave_number * jnp.sin(angles)
    phase_y = wave_y[:, None, None] * offset_grid[None]
    left_table = jnp.stack([envelope * jnp.cos(phase_y), envelope * jnp.sin(phase_y)], axis=2)
    left_table = left_table.reshape(orient * quarter * 2, quarter).astype(jnp.bfloat16)
    phase_x = wave_x[:, None, None] * (-offset_grid)[None]
    real_part = envelope * jnp.cos(phase_x)
    imag_part = envelope * jnp.sin(phase_x)
    upper_half = jnp.concatenate([real_part, imag_part], axis=2)
    lower_half = jnp.concatenate([-imag_part, real_part], axis=2)
    right_table = jnp.concatenate([upper_half, lower_half], axis=1).astype(jnp.bfloat16)
    return (left_table, right_table)


def phase_terms(coeffs, per_frame):
    quarter = coeffs.shape[-1] // 2
    coeff_real = coeffs[..., :quarter].astype(jnp.float32)
    coeff_imag = coeffs[..., quarter:].astype(jnp.float32)
    ref_real = per_frame[..., :quarter].astype(jnp.float32)
    ref_imag = per_frame[..., quarter:].astype(jnp.float32)
    prod_real = coeff_real * ref_real + coeff_imag * ref_imag
    prod_imag = coeff_imag * ref_real - coeff_real * ref_imag
    phase_signal = (
        prod_imag / jnp.sqrt(prod_real * prod_real + prod_imag * prod_imag + 1.0)
    ).astype(jnp.bfloat16)
    amplitude = coeff_real * coeff_real + coeff_imag * coeff_imag
    return (phase_signal, amplitude)


def taps_matrix(band_taps, frame_count):
    frame_index = jnp.arange(frame_count, dtype=jnp.int32)
    lag_grid = frame_index[:, None] - frame_index[None, :]
    one_hot = (
        lag_grid[:, :, None] == jnp.arange(band_taps.shape[0], dtype=jnp.int32)[None, None, :]
    ).astype(jnp.float32)
    return jnp.einsum("tsk,k->ts", one_hot, band_taps.astype(jnp.float32)).astype(jnp.bfloat16)


def segment_refs(segments, ref_pick, segment_count):
    numbers = jnp.arange(segment_count, dtype=jnp.int32)
    starts = jnp.sum((segments[None, :] < numbers[:, None]).astype(jnp.int32), axis=1)
    counts = jnp.sum((segments[None, :] == numbers[:, None]).astype(jnp.int32), axis=1)
    return starts + ref_pick % counts


def body(video_frames, segments, ref_pick, band_taps):
    frames_here = video_frames.shape[0]
    down_matrix = make_down(IMG, QUART)
    left_table, right_table = gabor_tables(QUART, ORIENT)

    def reduce_frames(pictures):
        half_done = jnp.einsum(
            "nia,qa->niq", pictures, down_matrix, preferred_element_type=jnp.float32
        ).astype(jnp.bfloat16)
        return jnp.einsum(
            "qi,nik->nqk", down_matrix, half_done, preferred_element_type=jnp.float32
        ).astype(jnp.bfloat16)

    def filter_frames(reduced):
        stacked = jnp.einsum(
            "ra,nak->nrk", left_table, reduced, preferred_element_type=jnp.float32
        ).astype(jnp.bfloat16)
        stacked = stacked.reshape(reduced.shape[0], ORIENT, QUART, 2 * QUART)
        return jnp.einsum(
            "noya,oab->noyb", stacked, right_table, preferred_element_type=jnp.float32
        ).astype(jnp.bfloat16)

    small_own = reduce_frames(video_frames)
    coeff_own = filter_frames(small_own)
    ref_frames = segment_refs(segments, ref_pick, NSEG)
    gathered = []
    for segment in range(NSEG):
        root_index = ref_frames[segment] // frames_here
        local_index = ref_frames[segment] % frames_here
        payload = lax.dynamic_index_in_dim(video_frames, local_index, 0, keepdims=False)
        gathered.append(spread(payload, "frames", root_index))
    ref_coeff = filter_frames(reduce_frames(jnp.stack(gathered)))
    first_frame = lax.axis_index("frames") * frames_here
    own_ids = lax.dynamic_slice_in_dim(segments, first_frame, frames_here)
    select = (own_ids[:, None] == jnp.arange(NSEG, dtype=jnp.int32)[None, :]).astype(jnp.bfloat16)
    per_frame = jnp.dot(select, ref_coeff.reshape(NSEG, -1), preferred_element_type=jnp.float32)
    per_frame = per_frame.astype(jnp.bfloat16).reshape(coeff_own.shape)
    phase_signal, amplitude = phase_terms(coeff_own, per_frame)
    phase_signal = phase_signal.reshape(frames_here, ORIENT, QUART * QUART)
    pixel_rows = lax.all_to_all(phase_signal, "frames", split_axis=2, concat_axis=0, tiled=True)
    matrix = taps_matrix(band_taps, pixel_rows.shape[0])
    filtered = jnp.einsum(
        "ts,sop->top", matrix, pixel_rows, preferred_element_type=jnp.float32
    ).astype(jnp.bfloat16)
    filtered = lax.all_to_all(filtered, "frames", split_axis=0, concat_axis=2, tiled=True)
    filtered = filtered.reshape(frames_here, ORIENT, QUART, QUART).astype(jnp.float32)
    return jnp.sum(amplitude * filtered, axis=1) / (jnp.sum(amplitude, axis=1) + 1.0)


PICK_LIMIT = 4096
REACH = 32


def down_table():
    position = np.arange(QUART, dtype=np.float32)[:, None]
    columns = np.arange(IMG, dtype=np.float32)[None, :]
    offset = columns - np.float32(4.0) * position - np.float32(1.5)
    weight = np.exp(-offset * offset / np.float32(2.0 * blur_sigma * blur_sigma))
    return (weight / np.sum(weight, axis=1, keepdims=True)).astype(jnp.bfloat16)


def waves():
    angles = np.arange(ORIENT, dtype=np.float32) * np.float32(math.pi / ORIENT)
    return np.float32(wave_number) * np.cos(angles), np.float32(wave_number) * np.sin(angles)


def gabor_envelope(offset):
    return np.float32(gabor_gain) * np.exp(-offset * offset / np.float32(2.0 * gabor_sigma * gabor_sigma))


def left_window(rows):
    offset = (
        np.arange(rows + 2 * REACH, dtype=np.float32)[None, :]
        - REACH
        - np.arange(rows, dtype=np.float32)[:, None]
    )
    envelope = gabor_envelope(offset)
    phase = waves()[1][:, None, None] * offset[None]
    table = np.stack([envelope * np.cos(phase), envelope * np.sin(phase)], axis=1)
    return table.reshape(ORIENT * 2 * rows, -1).astype(jnp.bfloat16)


def right_tables():
    position = np.arange(QUART, dtype=np.float32)
    offset = position[:, None] - position[None, :]
    envelope = gabor_envelope(offset)
    phase = waves()[0][:, None, None] * offset[None]
    real, imag = envelope * np.cos(phase), envelope * np.sin(phase)
    return np.stack([real, imag], axis=1).astype(jnp.bfloat16)


PLANE = 4
PAIR = 2
LAG = 3
DUE = 3
STRIP = 128
UNROLL = 4
ORDERS = ((0, 1, 2), (0, 1, 2))


def flip(number, bits):
    step = 1
    while step <= bits:
        if bits & step:
            number = number + step - 2 * step * ((number // step) % 2)
        step *= 2
    return number


def make_kernel(parts, here, rows):
    frames = parts * here
    planes = parts // PLANE
    window = rows + 2 * REACH
    pair_window = PAIR * rows + 2 * REACH
    total = frames * rows
    chunks = 2
    strips = QUART // STRIP

    def kernel(
        segments, picks, taps, video_hbm, down_hbm, down_t_hbm, left, right_hbm, out_hbm,
        video, down, down_t, right, half, column, beside, twin, stacked, coeffs,
        powers, phase, matrix, denom, moved,
        load_sem, store_sem, send_z, recv_z, send_l, recv_l, send_x, recv_x, send_c, recv_c, send_b, recv_b,
    ):
        me = lax.axis_index("frames")
        plane, spot = me // PLANE, me % PLANE
        across, sibling = flip(spot, PAIR), flip(spot, 1)
        side, core = spot // PAIR, spot % PAIR
        barrier = pltpu.get_barrier_semaphore()

        def peer(j):
            return lax.rem(me + j, parts)

        def piece(n, part):
            height = IMG // chunks
            where = pl.ds(part * height, height)
            return pltpu.make_async_copy(
                video_hbm.at[n, where], video.at[n, where], load_sem.at[3 + n * chunks + part]
            )

        load_down = pltpu.make_async_copy(down_hbm, down, load_sem.at[1])
        load_down_t = pltpu.make_async_copy(down_t_hbm, down_t, load_sem.at[0])
        load_right = pltpu.make_async_copy(right_hbm, right, load_sem.at[2])
        load_down_t.start()
        for n in range(here):
            for part in range(chunks):
                piece(n, part).start()
            if n == 0:
                load_down.start()
        load_right.start()

        def greet(where):
            pl.semaphore_signal(barrier, inc=1, device_id={"frames": where})

        others = [flip(plane, j) for j in range(1, planes)]
        for to in reversed(others):
            greet(to * PLANE + spot)
        greet(plane * PLANE + across)
        greet(plane * PLANE + sibling)

        blank = jnp.zeros((planes * here, REACH, QUART), jnp.bfloat16)
        column[:, :REACH, :] = blank
        column[:, REACH + QUART :, :] = blank

        block = PLANE * rows
        low, high = REACH, REACH + QUART

        def early(q):
            return 0 if q < max(planes // 2, 1) else 1

        ahead = side == jnp.where(plane < max(planes // 2, 1), 0, 1)

        def bounds(first, last):
            return max(first, low), min(last, high)

        def early_rows(q):
            first = block * q + (PAIR * rows if early(q) else 0)
            return bounds(first, first + pair_window)

        def late_rows(q):
            first = block * q + (0 if early(q) else pair_window)
            return bounds(first, first + PAIR * rows)

        def z_copy(f, n, q):
            first, last = early_rows(q)
            part = column.at[f * here + n, first:last, :]
            return pltpu.make_async_remote_copy(
                src_ref=part,
                dst_ref=part,
                send_sem=send_z.at[q, n],
                recv_sem=recv_z.at[f, n],
                device_id={"frames": q * PLANE + spot},
            )

        def z_part(f, n, to, act):
            for q in range(planes):

                @pl.when(to == q)
                def _():
                    act(z_copy(f, n, q))

        def z_send(n, to):
            z_part(plane, n, to, lambda copy: copy.start())

        def late_copy(f, n, q, straight):
            first, last = late_rows(q)
            inside = 0 if early(q) else pair_window - PAIR * rows
            inside = inside + first - (block * q + (0 if early(q) else pair_window))
            target = (
                column.at[f * here + n, first:last, :]
                if straight
                else beside.at[f * here + n, inside : inside + last - first, :]
            )
            other_side = 1 - early(q)
            return pltpu.make_async_remote_copy(
                src_ref=column.at[f * here + n, first:last, :],
                dst_ref=target,
                send_sem=send_l.at[q, n],
                recv_sem=recv_l.at[0 if straight else 1, f, n],
                device_id={"frames": q * PLANE + other_side * PAIR + core},
            )

        def has_late(q):
            first, last = late_rows(q)
            return last > first

        def late_own(n, act):
            for q in range(planes):
                if has_late(q):

                    @pl.when((side == 1 - early(q)) & (plane != q))
                    def _():
                        act(late_copy(plane, n, q, True))

                    @pl.when(side == early(q))
                    def _():
                        act(late_copy(plane, n, q, False))

        def late_wait(f, n, straight):
            for q in range(planes):
                if has_late(q):

                    @pl.when(plane == q)
                    def _():
                        late_copy(f, n, q, straight).wait_recv()

        def x_copy(f, n, q, whole):
            first = block * q + (PAIR * rows if early(q) else 0)
            inside, size = 0, pair_window
            if not whole:
                first, size = block * q + PAIR * rows, pair_window - PAIR * rows
                inside = PAIR * rows if early(q) else 0
            return pltpu.make_async_remote_copy(
                src_ref=column.at[f * here + n, first : first + size, :],
                dst_ref=beside.at[f * here + n, inside : inside + size, :],
                send_sem=send_x.at[f, n],
                recv_sem=recv_x.at[f, n],
                device_id={"frames": plane * PLANE + across},
            )

        def x_each(f, n, to_ahead, act):
            for q in range(planes):
                for whole in (False, True):

                    @pl.when((plane == q) & (to_ahead == whole))
                    def _():
                        act(x_copy(f, n, q, whole))

        def x_send(f, n):
            x_each(f, n, ~ahead, lambda copy: copy.start())

        def core_copy(f, n):
            first = pl.multiple_of(plane * block + sibling * rows, rows)
            return pltpu.make_async_remote_copy(
                src_ref=column.at[f * here + n, pl.ds(first, window), :],
                dst_ref=twin.at[0, f * here + n],
                send_sem=send_c.at[0, f, n],
                recv_sem=recv_c.at[0, f, n],
                device_id={"frames": plane * PLANE + sibling},
            )

        def pass_copy(f, n):
            first = pl.multiple_of((1 - core) * rows, rows)
            return pltpu.make_async_remote_copy(
                src_ref=beside.at[f * here + n, pl.ds(first, window), :],
                dst_ref=twin.at[1, f * here + n],
                send_sem=send_c.at[1, f, n],
                recv_sem=recv_c.at[1, f, n],
                device_id={"frames": plane * PLANE + sibling},
            )

        load_down_t.wait()
        for n in range(here):
            for part in range(chunks):
                piece(n, part).wait()
                where = slice(part * (IMG // chunks), (part + 1) * (IMG // chunks))
                half[n, where] = jnp.dot(
                    video[n, where], down_t[...], preferred_element_type=jnp.float32
                ).astype(jnp.bfloat16)
            if n == 0:
                load_down.wait()
            column[plane * here + n, REACH : REACH + QUART, :] = jnp.dot(
                down[...], half[n], preferred_element_type=jnp.float32
            ).astype(jnp.bfloat16)
            if n == 0:
                pl.semaphore_wait(barrier, planes + 1)
            x_send(plane, n)
            core_copy(plane, n).start()
            for i in ORDERS[min(n, 1)]:
                if i < planes - 1:
                    z_send(n, others[i])

        counts = [jnp.int32(0)] * NSEG
        for t in range(frames):
            for s in range(NSEG):
                counts[s] = counts[s] + jnp.where(segments[t] == s, 1, 0)
        picked, first = [], jnp.int32(0)
        for s in range(NSEG):
            rest = picks[s]
            for bit in reversed(range((PICK_LIMIT - 1).bit_length())):
                rest = jnp.where(rest >= counts[s] * (1 << bit), rest - counts[s] * (1 << bit), rest)
            picked.append(first + rest)
            first = first + counts[s]

        lag = lax.broadcasted_iota(jnp.int32, (frames, frames), 0) - lax.broadcasted_iota(
            jnp.int32, (frames, frames), 1
        )
        toeplitz = jnp.zeros((frames, frames), jnp.float32)
        tap_row = taps[...].astype(jnp.float32)
        for k in range(min(taps.shape[1], frames)):
            toeplitz = jnp.where(lag == k, tap_row[:, k : k + 1], toeplitz)
        owner = lax.broadcasted_iota(jnp.int32, (total, frames), 0) // rows
        repeat = jnp.where(
            owner == lax.broadcasted_iota(jnp.int32, (total, frames), 1), 1.0, 0.0
        ).astype(jnp.bfloat16)
        tall = jnp.dot(
            repeat, toeplitz.astype(jnp.bfloat16), preferred_element_type=jnp.float32
        ).astype(jnp.bfloat16)
        wide = lax.dot_general(
            tall, repeat, (((1,), (1,)), ((), ())), preferred_element_type=jnp.float32
        )
        same = (
            lax.broadcasted_iota(jnp.int32, (total, total), 0) % rows
            == lax.broadcasted_iota(jnp.int32, (total, total), 1) % rows
        )
        matrix[...] = jnp.where(same, wide, 0.0).astype(jnp.bfloat16)

        def stack_one(place, block):
            stacked[place] = (
                jnp.dot(left[...], block, preferred_element_type=jnp.float32)
                .astype(jnp.bfloat16)
                .reshape(ORIENT * 2, rows, QUART)
            )

        def coefficients(where):
            tall_rows = planes * here * rows
            total_power = [0.0] * strips
            for o in range(ORIENT):
                even = stacked[:, where, :, 2 * o].reshape(tall_rows, QUART)
                odd = stacked[:, where, :, 2 * o + 1].reshape(tall_rows, QUART)

                def times(left_part, which):
                    return jnp.dot(left_part, right[o, which], preferred_element_type=jnp.float32)

                real = (times(even, 0) - times(odd, 1)).astype(jnp.bfloat16)
                imag = (times(even, 1) + times(odd, 0)).astype(jnp.bfloat16)
                wide_real, wide_imag = real.astype(jnp.float32), imag.astype(jnp.float32)
                power = wide_real * wide_real + wide_imag * wide_imag
                slot = slice(o % 2 * STRIP, (o % 2 + 1) * STRIP)
                imag_slot = slice(QUART + o % 2 * STRIP, QUART + (o % 2 + 1) * STRIP)
                for h in range(strips):
                    columns = slice(h * STRIP, (h + 1) * STRIP)
                    total_power[h] = total_power[h] + power[:, columns]

                    def split(value):
                        return value[:, columns].reshape(planes, here, rows, STRIP)

                    for p in range(planes):
                        at = pl.ds((p * PLANE + where) * here, here)
                        coeffs[h, at, o // 2, :, slot] = split(real)[p]
                        coeffs[h, at, o // 2, :, imag_slot] = split(imag)[p]
                        powers[h, at, o // 2, :, slot] = split(power)[p]
            for h in range(strips):
                whole = (total_power[h] + 1.0).reshape(planes, here, rows, STRIP)
                for p in range(planes):
                    denom[h, pl.ds((p * PLANE + where) * here, here)] = whole[p]

        own_rows = pl.ds(pl.multiple_of(plane * block + spot * rows, rows), window)
        core_rows = pl.ds(pl.multiple_of(core * rows, rows), window)

        def stack_column(f, n):
            stack_one((f, spot, n), column[f * here + n, own_rows, :])

        def stack_twin(f, n):
            stack_one((f, sibling, n), twin[0, f * here + n])

        def stack_sibling(f, n):
            core_copy(f, n).wait_recv()
            stack_twin(f, n)

        def x_wait(f, n):
            x_each(f, n, ahead, lambda copy: copy.wait_recv())

        def stack_beside(f, n):
            stack_one((f, across, n), beside[f * here + n, core_rows, :])

        def stack_passed(f, n):
            stack_one((f, flip(across, 1), n), twin[1, f * here + n])

        def stack_across(f, n):
            pass_copy(f, n).start()
            stack_beside(f, n)

        def stack_last(f, n):
            pass_copy(f, n).wait_recv()
            stack_passed(f, n)

        events = [(plane, n) for n in range(here)] + [
            (others[i], n)
            for n in range(here)
            for i in ORDERS[min(n, 1)]
            if i < planes - 1
        ]
        held_back = len(events) - LAG
        for i, (f, n) in enumerate(events):
            if i >= here:
                z_part(f, n, plane, lambda copy: copy.wait_recv())
                x_send(f, n)

                @pl.when(ahead)
                def _():
                    core_copy(f, n).start()

            if i == min(LAG, DUE):
                x_wait(*events[0])
            if i == DUE:
                for m in range(here):
                    late_own(m, lambda copy: copy.start())

            if i < here:
                stack_column(f, n)
            if 1 <= i <= here:
                stack_sibling(*events[i - 1])

            @pl.when(ahead)
            def _():
                if i >= here:
                    stack_column(f, n)
                if i > here:
                    stack_sibling(*events[i - 1])
                if i >= LAG:
                    if i > LAG:
                        x_wait(*events[i - LAG])
                    stack_across(*events[i - LAG])
                if i >= LAG + 1:
                    stack_last(*events[i - LAG - 1])

        @pl.when(~ahead)
        def _():
            middle = here + planes - 1
            for group in (range(middle), range(middle, len(events))):
                forward = [i for i in group if i < held_back]
                for i in group:
                    if i >= here:
                        late_wait(*events[i], True)
                        core_copy(*events[i]).start()
                for i in forward:
                    if i:
                        x_wait(*events[i])
                    late_wait(*events[i], False)
                    pass_copy(*events[i]).start()
                for i in group:
                    if i >= here:
                        stack_column(*events[i])
                for i in forward:
                    stack_beside(*events[i])
                twins = [i for i in group if here <= i < len(events) - 1]
                for i in twins:
                    core_copy(*events[i]).wait_recv()
                for i in twins:
                    stack_twin(*events[i])
                ready = [i for i in forward if i < held_back - 1]
                for i in ready:
                    pass_copy(*events[i]).wait_recv()
                for i in ready:
                    stack_passed(*events[i])

        stack_sibling(*events[-1])
        load_right.wait()
        coefficients(spot)
        coefficients(sibling)
        for f, n in events[held_back:]:
            x_wait(f, n)

            @pl.when(~ahead)
            def _():
                late_wait(f, n, False)

            pass_copy(f, n).start()
        for event in events[held_back:]:
            stack_beside(*event)
        coefficients(across)
        for f, n in events[held_back - 1 :]:
            pass_copy(f, n).wait_recv()
        for event in events[held_back - 1 :]:
            stack_passed(*event)
        coefficients(flip(across, 1))

        here_rows = pl.ds(pl.multiple_of(me * rows, rows), rows)

        def phases(h):
            @pl.loop(0, frames // UNROLL)
            def _(step):
                for u in range(UNROLL):
                    t = step * UNROLL + u
                    ref = picked[NSEG - 1]
                    for s in range(NSEG - 1):
                        ref = jnp.where(segments[t] == s, picked[s], ref)
                    ones = coeffs[h, t].astype(jnp.float32)
                    base = coeffs[h, ref].astype(jnp.float32)
                    prod_imag = ones[..., QUART:] * base[..., :QUART] - ones[..., :QUART] * base[..., QUART:]
                    signal = prod_imag * lax.rsqrt(powers[h, t] * powers[h, ref] + 1.0)
                    phase[:, t] = signal.astype(jnp.bfloat16)

        def return_copy(h, j):
            to = peer(j)
            return pltpu.make_async_remote_copy(
                src_ref=moved.at[h, pl.ds(to * here, here)],
                dst_ref=out_hbm.at[:, here_rows, h * STRIP : (h + 1) * STRIP],
                send_sem=send_b.at[h, j],
                recv_sem=recv_b.at[h, j],
                device_id={"frames": to},
            )

        def store(h):
            return pltpu.make_async_copy(
                moved.at[h, pl.ds(me * here, here)],
                out_hbm.at[:, here_rows, h * STRIP : (h + 1) * STRIP],
                store_sem.at[h],
            )

        crowd = parts // 2
        near = me // crowd

        def filter_half(h, number):
            span = slice(number * (frames // 2), (number + 1) * (frames // 2))
            until = (number + 1) * (total // 2)
            numer = 0.0
            for q in range(ORIENT // 2):
                filtered = (
                    jnp.dot(
                        matrix[number * (total // 2) : until, :until],
                        phase[q].reshape(total, QUART)[:until],
                        preferred_element_type=jnp.float32,
                    )
                    .astype(jnp.bfloat16)
                    .astype(jnp.float32)
                    .reshape(frames // 2, rows, QUART)
                )
                numer = numer + powers[h, span, q] * filtered
            numer = numer[..., :STRIP] + numer[..., STRIP:]
            moved[h, span] = (numer / denom[h, span]).astype(jnp.bfloat16)

        for h in range(strips):
            phases(h)
            for close in (False, True):
                for number in range(2):

                    @pl.when((near == number) == close)
                    def _():
                        filter_half(h, number)

                base_to = (near if close else 1 - near) * crowd

                @pl.loop(1 if close else 0, crowd)
                def _(k):
                    to = base_to + lax.rem(me + k, crowd)
                    return_copy(h, lax.rem(to + parts - me, parts)).start()

            store(h).start()

        for f, n in events:
            x_each(f, n, ~ahead, lambda copy: copy.wait_send())
            core_copy(f, n).wait_send()
            pass_copy(f, n).wait_send()
        for n in range(here):
            for to in others:
                z_part(plane, n, to, lambda copy: copy.wait_send())
            late_own(n, lambda copy: copy.wait_send())

        for h in range(strips):

            @pl.loop(1, parts)
            def _(j):
                return_copy(h, j).wait_recv()
                return_copy(h, j).wait_send()

            store(h).wait()

    bf16, f32, dma = jnp.bfloat16, jnp.float32, pltpu.SemaphoreType.DMA
    anywhere = pl.BlockSpec(memory_space=pl.ANY)
    vmem = pl.BlockSpec(memory_space=pltpu.VMEM)
    smem = pl.BlockSpec(memory_space=pltpu.SMEM)
    return pl.pallas_call(
        kernel,
        out_shape=jax.ShapeDtypeStruct((here, QUART, QUART), bf16),
        in_specs=[smem, smem, vmem, anywhere, anywhere, anywhere, vmem, anywhere],
        out_specs=anywhere,
        scratch_shapes=[
            pltpu.VMEM((here, IMG, IMG), bf16),
            pltpu.VMEM((QUART, IMG), bf16),
            pltpu.VMEM((IMG, QUART), bf16),
            pltpu.VMEM((ORIENT, 2, QUART, QUART), bf16),
            pltpu.VMEM((here, IMG, QUART), bf16),
            pltpu.VMEM((planes * here, QUART + 2 * REACH, QUART), bf16),
            pltpu.VMEM((planes * here, pair_window, QUART), bf16),
            pltpu.VMEM((2, planes * here, window, QUART), bf16),
            pltpu.VMEM((planes, PLANE, here, ORIENT * 2, rows, QUART), bf16),
            pltpu.VMEM((strips, frames, ORIENT // 2, rows, 2 * QUART), bf16),
            pltpu.VMEM((strips, frames, ORIENT // 2, rows, QUART), f32),
            pltpu.VMEM((ORIENT // 2, frames, rows, QUART), bf16),
            pltpu.VMEM((total, total), bf16),
            pltpu.VMEM((strips, frames, rows, STRIP), f32),
            pltpu.VMEM((strips, frames, rows, STRIP), bf16),
            dma((3 + here * chunks,)),
            dma((strips,)),
            dma((planes, here)),
            dma((planes, here)),
            dma((planes, here)),
            dma((2, planes, here)),
            dma((planes, here)),
            dma((planes, here)),
            dma((2, planes, here)),
            dma((2, planes, here)),
            dma((strips, parts)),
            dma((strips, parts)),
        ],
        compiler_params=pltpu.CompilerParams(
            collective_id=0, has_side_effects=True, vmem_limit_bytes=60 * 1024 * 1024
        ),
    )


def kernel_body(parts, video_frames, segments, ref_pick, band_taps):
    here = video_frames.shape[0]
    rows = QUART // parts
    down = down_table()
    return make_kernel(parts, here, rows)(
        segments,
        ref_pick,
        band_taps[None, :],
        video_frames,
        jnp.asarray(down),
        jnp.asarray(np.ascontiguousarray(down.T)),
        jnp.asarray(left_window(rows)),
        jnp.asarray(right_tables()),
    ).astype(jnp.float32)


def solution(mesh):
    parts = mesh.shape["frames"]
    if QUART % parts == 0 and (QUART // parts) % 16 == 0 and parts in (4, 8, 16):
        chosen = lambda *args: kernel_body(parts, *args)
    else:
        chosen = body
    in_specs = (P(("groups", "frames"), None, None), P("groups"), P("groups"), P())
    out_specs = P(("groups", "frames"), None, None)
    return jax.shard_map(chosen, mesh=mesh, in_specs=in_specs, out_specs=out_specs, check_vma=False)
```
